512 devices in a mesh: tile: 64 (over z, y_lo, core), head: 8 (over x, y_hi).
Axes of the slice: x: 4, y: 4 (y_hi: 2, y_lo: 2; y = y_hi * 2 + y_lo), z: 16, core: 2. Of those that a mesh axis runs over, the one named last changes fastest.
Arguments:
- query_rows: bfloat16 [24576, 5120], P('tile', 'head'), may hold values from -60 to 60
- key_rows: bfloat16 [24576, 5120], P('tile', 'head'), may hold values from -60 to 60
- value_rows: bfloat16 [24576, 5120], P('tile', 'head'), may hold values from -6 to 6
- gain_q: float32 [5120], P('head'), may hold values from 0.1 to 1.9
- gain_k: float32 [5120], P('head'), may hold values from 0.1 to 1.9
- mem_keys: bfloat16 [1024, 8, 5120], P('tile', None, 'head'), may hold values from -6 to 6
- mem_values: bfloat16 [1024, 8, 5120], P('tile', None, 'head'), may hold values from -6 to 6
- tile_len: int32 [64], P('tile'), may hold values from 1 to 384, 18432 in all
- session: int32 [64], P('tile'), may hold values from 0 to 5, never falling along the last dimension, each value on 1 to 17 neighbouring positions
- req_owner: int32 [4096, 1], P('tile'), may hold values from 0 to 63; in each aligned block of 64 rows (0 to 63, 64 to 127, ...) at most 2 rows name the same one
- requested_block_index: int32 [4096], P('tile'), may hold values from 0 to 15
Outputs:
- attended: bfloat16 [24576, 5120], P('tile', 'head')
The draws below stay inside these ranges and needn't reach their ends.
Inputs may be any that keep to these rules, and one draw needn't show every extreme that they name: Each session's tiles stand in a row, the session numbers never falling along tiles; a session has 1 to 17 tiles. `req_owner`: among the 64 requests of one tile at most 2 name the same owner, and exactly 2 do for some owner and tile.
All inputs are finite; a program needn't handle non-finite values. No bound on the sum of `tile_len` on one device may be relied on, other than what follows from the above.
Results may differ from the reference program's by a relative error of at most 0.011.
Values may be sent and summed in bfloat16 or wider, within the bound.
A program may use at most 64 MiB of HBM per device.

```python
import math
import jax
import jax.numpy as jnp
import numpy as np
from jax import lax

HEADS = 40
HEAD_DIM = 128
WIDTH = 5120
TILE_CAP = 384
EDGE = 64
BLOCK = 8
RETR = 64
BLK_DEV = 16
SESSIONS = 6
N_TILE_SEG = 17
SLOT = 2
TOKENS = 24576
MEMB = 1024
RTOT = 4096
N_TILE = 64


def shared_fields(key):
    keys_all = jax.random.split(jax.random.fold_in(key, 17), 5)
    base_query = jax.random.normal(keys_all[0], (TOKENS, WIDTH), jnp.float32)
    base_key = jax.random.normal(keys_all[1], (TOKENS, WIDTH), jnp.float32)
    column_pos = jnp.arange(WIDTH, dtype=jnp.float32) / WIDTH
    column_scale = 0.6 * 3.0 ** column_pos * jnp.exp(jax.random.uniform(keys_all[2], (WIDTH,), jnp.float32, -0.7, 0.7))
    row_query = 0.4 * jnp.exp(jax.random.uniform(keys_all[3], (TOKENS, 1), jnp.float32, 0.0, 2.3))
    row_key = 0.4 * jnp.exp(jax.random.uniform(keys_all[4], (TOKENS, 1), jnp.float32, 0.0, 2.3))
    query_field = jnp.clip(base_query * row_query * column_scale[None, :], -60.0, 60.0)
    key_field = jnp.clip(base_key * row_key * column_scale[None, :], -60.0, 60.0)
    return (query_field, key_field)


def draw_query_rows(key, part):
    query_field, key_field = shared_fields(key)
    return query_field.astype(jnp.bfloat16)


def draw_key_rows(key, part):
    query_field, key_field = shared_fields(key)
    return key_field.astype(jnp.bfloat16)


def plant(values, own_key, smallest, high):
    place = [jax.random.randint(jax.random.fold_in(own_key, axis), (), 0, length) for axis, length in enumerate(values.shape)]
    longest = values.shape.index(max(values.shape))
    neighbour = place[:longest] + [(place[longest] + 1) % values.shape[longest]] + place[longest + 1:]
    return values.at[tuple(place)].set(smallest).at[tuple(neighbour)].set(high)


def block_levels(key, extent, shards, low, top_value):
    def one(dim, parts):
        heights = jax.random.uniform(jax.random.fold_in(jax.random.fold_in(key, 6), dim), (parts,), jnp.float32, low / len(shards), top_value / len(shards))
        return jnp.repeat(jnp.exp(heights), extent[dim] // parts).reshape((-1,) + (1,) * (len(extent) - dim - 1))

    level = one(*shards[0])
    for cut in shards[1:]:
        level = level * one(*cut)
    return level


def split_up(amount, total, most, skew):
    loads = [(1 << 20) // math.isqrt(standing ** skew) + 1 for standing in range(2, amount + 1)]
    spare, holding = total - most - (amount - 1), [1] * (amount - 1)
    while spare > 0:
        candidates = [i for i in range(amount - 1) if holding[i] < most]
        whole, budget = sum([loads[i] for i in candidates]), spare
        for i in candidates:
            extra = min(most - holding[i], max(1, budget * loads[i] // whole), spare)
            holding[i] = holding[i] + extra
            spare = spare - extra
    return np.array([most] + holding)


def uneven(own_key, number_of, total, limit, skew):
    if number_of == 2:
        one = jax.random.randint(own_key, (), max(1, total - limit), min(limit, total - 1) + 1)
        return jnp.stack([one, total - one])
    lengths = jnp.asarray(split_up(number_of, total, limit, skew), jnp.int32)
    pairs = (number_of - 1) // 2
    giver, taker = lengths[1:1 + 2 * pairs:2], lengths[2:2 + 2 * pairs:2]
    room = jnp.minimum(giver - 1, limit - taker)
    passed = jax.random.randint(jax.random.fold_in(own_key, 1), (pairs,), 0, 1 << 20) % (room + 1)
    lengths = lengths.at[1:1 + 2 * pairs:2].set(giver - passed).at[2:2 + 2 * pairs:2].set(taker + passed)
    return lengths[jax.random.permutation(jax.random.fold_in(own_key, 2), number_of)]


def routed_block(stream_key, own, number, rows, count, top, limit, slope):
    sequence = jax.random.permutation(stream_key, count)
    crowded, usual = shares(count, rows * top, limit, slope, True), shares(count, rows * top, limit, slope, False)
    places = jnp.arange(count)

    def named(lengths, rotation):
        used = int((lengths > 0).sum())
        fixed = max(1, used // 4)
        passed = fixed + (places - fixed + rotation * (used - fixed)) % max(1, count - fixed)
        return jnp.zeros((count,), jnp.int32).at[sequence[jnp.where(places < fixed, places, passed)]].set(jnp.asarray(lengths, jnp.int32))

    lengths = jnp.where(number % 4 == 0, named(crowded, number // 4), named(usual, number - number // 4 - 1))
    mixed = jax.random.permutation(jax.random.fold_in(own, 3), count)
    source_of, taker = mixed[0:count // 2 * 2:2], mixed[1:count // 2 * 2:2]
    margin = jnp.minimum(lengths[source_of] - 1, limit - lengths[taker]) // 2
    margin = jnp.where((source_of == sequence[0]) | (taker == sequence[0]) | (lengths[taker] == 0), 0, jnp.maximum(margin, 0))
    passed = jax.random.randint(jax.random.fold_in(own, 4), (count // 2,), 0, 1 << 20) % (margin + 1)
    lengths = lengths.at[source_of].add(-passed).at[taker].add(passed)
    items = jnp.searchsorted(jnp.cumsum(lengths), jnp.arange(rows * top), side="right").astype(jnp.int32)
    grid = items.reshape(top, rows).T
    grid = grid[jax.random.permutation(jax.random.fold_in(own, 1), rows)]
    rotation = jax.random.randint(jax.random.fold_in(own, 2), (rows, 1), 0, top)
    return jnp.take_along_axis(grid, (jnp.arange(top)[None, :] + rotation) % top, axis=1)


def shares(count, total, most, skew, full):
    loads = [(1 << 20) // math.isqrt(standing ** skew) + 1 for standing in range(1, count + 1)]
    largest = most if full else min(most, max(-(-total // count), total * loads[0] // sum(loads)))
    least = 1 if total - largest >= count - 1 else 0
    given, surplus = [largest] + [least] * (count - 1), total - largest - least * (count - 1)
    while surplus > 0:
        free = [i for i in range(1, count) if given[i] < largest] or [i for i in range(1, count) if given[i] < most]
        mass, budget = sum([loads[i] for i in free]), surplus
        for i in free:
            more = min(most - given[i], max(1, budget * loads[i] // mass), surplus)
            given[i] = given[i] + more
            surplus = surplus - more
    return np.array(given)


def normal_values(rng, shape, deviation, most, shards=(), kind=jnp.bfloat16):
    values = jax.random.normal(rng, shape, jnp.float32) * deviation
    if len(shards) > 0:
        values = block_levels(rng, shape, shards, -0.22, 0.18) * values
    return jnp.clip(values, min=-most, max=most).astype(kind)


def setup_inputs(seed: int = 0) -> dict:
    keys = jax.random.split(jax.random.key(seed), 12)
    query_rows = draw_query_rows(jax.random.fold_in(keys[11], 71), 0)
    key_rows = draw_key_rows(jax.random.fold_in(keys[11], 71), 0)
    value_rows = normal_values(keys[2], (TOKENS, WIDTH), 1.0, 6.0, ((0, 64), (1, 8)))
    gain_q = jnp.clip(1.0 + 0.18 * jax.random.normal(keys[3], (WIDTH,), jnp.float32), 0.1, 1.9)
    gain_k = jnp.clip(1.0 + 0.18 * jax.random.normal(keys[4], (WIDTH,), jnp.float32), 0.1, 1.9)
    mem_keys = normal_values(keys[5], (MEMB, BLOCK, WIDTH), 1.0, 6.0, ((0, 64), (2, 8)))
    mem_values = normal_values(keys[6], (MEMB, BLOCK, WIDTH), 1.0, 6.0, ((0, 64), (2, 8)))
    tile_len = uneven(keys[7], N_TILE, N_TILE * TILE_CAP * 3 // 4, TILE_CAP, 2).astype(jnp.int32)
    session = jnp.searchsorted(jnp.cumsum(uneven(keys[8], SESSIONS, N_TILE, N_TILE_SEG, 1)), jnp.arange(N_TILE), side="right").astype(jnp.int32)
    req_owner_keys = jax.random.split(jax.random.fold_in(keys[9], 1), RTOT // RETR)
    req_owner_turns = jax.random.permutation(jax.random.fold_in(keys[9], 3), RTOT // RETR)
    req_owner = jax.vmap(lambda own, number: routed_block(jax.random.fold_in(keys[9], 2), own, number, RETR, N_TILE, 1, SLOT, 2))(req_owner_keys, req_owner_turns).reshape((RTOT, 1))
    requested_block_index = plant(jax.random.randint(keys[10], (RTOT,), 0, BLK_DEV), jax.random.fold_in(keys[10], 1), 0, BLK_DEV - 1).astype(jnp.int32)
    return {"query_rows": query_rows, "key_rows": key_rows, "value_rows": value_rows, "gain_q": gain_q, "gain_k": gain_k, "mem_keys": mem_keys, "mem_values": mem_values, "tile_len": tile_len, "session": session, "req_owner": req_owner, "requested_block_index": requested_block_index}


EPSILON = 1e-06

def norm_rows(raw_rows, gain):
    rows32 = raw_rows.astype(jnp.float32)
    mean_sq = lax.optimization_barrier(jnp.sum(rows32 * rows32, axis=-1, keepdims=True)) / WIDTH
    return (rows32 * lax.rsqrt(mean_sq + EPSILON) * gain.astype(jnp.float32)).astype(jnp.bfloat16)

def reference(query_rows, key_rows, value_rows, gain_q, gain_k, mem_keys, mem_values, tile_len, session, req_owner, requested_block_index):
    wanted = (req_owner[:, 0] * BLK_DEV + requested_block_index).astype(jnp.int32).reshape(N_TILE, RETR)
    edge_index = jnp.arange(EDGE, dtype=jnp.int32)
    slot_index = jnp.arange(TILE_CAP, dtype=jnp.int32)
    score_scale = 1.0 / HEAD_DIM ** 0.5

    def tile_rows(source, which):
        return lax.dynamic_slice_in_dim(source, (which * TILE_CAP).astype(jnp.int32), TILE_CAP, 0)

    def one_tile(which):
        before = jnp.maximum(which - 1, 0).astype(jnp.int32)
        after = jnp.minimum(which + 1, N_TILE - 1).astype(jnp.int32)
        query_norm = norm_rows(tile_rows(query_rows, which), gain_q)
        own_keys = norm_rows(tile_rows(key_rows, which), gain_k)
        own_values = tile_rows(value_rows, which)
        left_keys = norm_rows(tile_rows(key_rows, before), gain_k)
        left_values = tile_rows(value_rows, before)
        right_keys = norm_rows(tile_rows(key_rows, after), gain_k)
        right_values = tile_rows(value_rows, after)
        blank = jnp.zeros((EDGE, WIDTH), jnp.bfloat16)
        left_len = tile_len[before].astype(jnp.int32)
        tail_keys = lax.dynamic_slice_in_dim(jnp.concatenate([blank, left_keys], 0), left_len, EDGE, 0)
        tail_values = lax.dynamic_slice_in_dim(jnp.concatenate([blank, left_values], 0), left_len, EDGE, 0)
        left_ok = (which > 0) & (session[before] == session[which]) & (edge_index >= EDGE - left_len)
        right_ok = (which < N_TILE - 1) & (session[after] == session[which]) & (edge_index < tile_len[after])
        own_ok = slot_index < tile_len[which]
        memory_keys = jnp.take(mem_keys, wanted[which], axis=0).reshape(RETR * BLOCK, WIDTH)
        memory_values = jnp.take(mem_values, wanted[which], axis=0).reshape(RETR * BLOCK, WIDTH)
        all_keys = jnp.concatenate([own_keys, tail_keys, right_keys[:EDGE], memory_keys], 0)
        all_values = jnp.concatenate([own_values, tail_values, right_values[:EDGE], memory_values], 0)
        visible = jnp.concatenate([own_ok, left_ok, right_ok, jnp.ones((RETR * BLOCK,), bool)], 0)
        query32 = query_norm.astype(jnp.float32).reshape(TILE_CAP, HEADS, HEAD_DIM)
        key32 = all_keys.astype(jnp.float32).reshape(-1, HEADS, HEAD_DIM)
        value32 = all_values.astype(jnp.float32).reshape(-1, HEADS, HEAD_DIM)
        scores = jnp.einsum('qhd,khd->hqk', query32, key32) * score_scale
        scores = jnp.where(visible[None, None, :], scores, jnp.float32(-1e+30))
        top = lax.optimization_barrier(jnp.max(scores, axis=-1, keepdims=True))
        expo = jnp.exp(scores - top)
        weights = (expo / lax.optimization_barrier(jnp.sum(expo, axis=-1, keepdims=True))).astype(jnp.bfloat16)
        result = jnp.einsum('hqk,khd->qhd', weights.astype(jnp.float32), value32).reshape(TILE_CAP, WIDTH)
        return jnp.where(own_ok[:, None], result, jnp.float32(0.0)).astype(jnp.bfloat16)
    tiles_out = lax.map(one_tile, jnp.arange(N_TILE, dtype=jnp.int32))
    return tiles_out.reshape(TOKENS, WIDTH)
```

```python
import functools
import math

import jax
import jax.numpy as jnp
from jax import lax
from jax.experimental import pallas as pl
from jax.experimental.pallas import tpu as pltpu
from jax.sharding import PartitionSpec as P

HEAD_DIM = 128
EDGE = 64
EPSILON = 1e-06
MESH = pl.DeviceIdType.MESH
NEG = -1e30
BF16 = jnp.bfloat16
F32 = jnp.float32
SCORE_SCALE = (1.0 / HEAD_DIM**0.5) * math.log2(math.e)


def kernel(
    tiles, nh, width,
    len_ref, ses_ref, own_ref, idx_ref, gq_ref, gk_ref,
    q_hbm, k_hbm, v_hbm, mk_hbm, mv_hbm, o_ref,
    kb, vb, cur_ka, cur_va, cur_kb, cur_vb,
    qr, kr, vr, qn, kn,
    ssrc, sbuf, wsrc, wrecv, mrecv, wsm,
    tail_k, tail_v, ek, ev,
    selk, selv, mkk, mvv,
    acc, mx, ls,
    rss, rrs, loc, sss, srs, wss, wrs, wls, mss, mrs, ess, ers, pss, prs,
):
    nz, half = tiles // 4, tiles // 8
    cap, wid = qr.shape
    heads = wid // HEAD_DIM
    t, h = lax.axis_index("tile"), lax.axis_index("head")
    z, sub = t // 4, lax.rem(t, 4)
    up, dn = lax.rem(t + 4, tiles), lax.rem(t + tiles - 4, tiles)
    right, left = lax.rem(t + 1, tiles), lax.rem(t + tiles - 1, tiles)

    def near(rel):
        other = sub + jnp.where(lax.rem(sub, 2) == 0, 1, -1) * (rel % 2)
        other = other + jnp.where(sub // 2 == 0, 2, -2) * (rel // 2)
        return z * 4 + other

    bar = pltpu.get_barrier_semaphore()
    greet = [up, dn, near(1), near(2), near(3), right, left]
    for n in greet:
        pl.semaphore_signal(bar, inc=1, device_id={"tile": n}, device_id_type=MESH)
    for i in range(1, nh):
        pl.semaphore_signal(bar, inc=1, device_id={"head": lax.rem(h + i, nh)}, device_id_type=MESH)
    pl.semaphore_wait(bar, len(greet) + nh - 1)

    def hop(d, s, x):
        buf, first = ((kb, mk_hbm), (vb, mv_hbm))[x]
        static = isinstance(s, int)
        if d == 0:
            src, dst, dev = s - 1, s, up
        else:
            src, dst, dev = nz + 1 - s, nz - s, dn
        return pltpu.make_async_remote_copy(
            src_ref=first if static and s == 1 else buf.at[src], dst_ref=buf.at[dst],
            send_sem=rss.at[d, s - 1, x], recv_sem=rrs.at[d, s - 1, x],
            device_id={"tile": dev}, device_id_type=MESH)

    for x in range(2):
        for d in range(2):
            hop(d, 1, x).start()

    loads = [
        pltpu.make_async_copy(a, b, loc.at[i])
        for i, (a, b) in enumerate(
            ((q_hbm, qr), (k_hbm, kr), (mk_hbm, kb.at[0]), (mv_hbm, vb.at[0]), (v_hbm, vr))
        )
    ]
    for copy in loads:
        copy.start()

    lane = lax.broadcasted_iota(jnp.int32, (1, 128), 1)

    def ask(r, carry):
        w0, w1 = carry
        hit, b = lane == own_ref[r], idx_ref[r]
        return (
            jnp.where(jnp.logical_and(hit, w0 < 0), b, w0),
            jnp.where(jnp.logical_and(hit, w0 >= 0), b, w1),
        )

    none = jnp.full((1, 128), -1, jnp.int32)
    w0, w1 = lax.fori_loop(0, own_ref.shape[0], ask, (none, none))
    length, session = len_ref[0], ses_ref[0]
    wsrc[0:1, :] = w0
    wsrc[1:2, :] = w1
    wsrc[2:3, :] = jnp.full((1, 128), length, jnp.int32)
    wsrc[3:4, :] = jnp.full((1, 128), session, jnp.int32)
    wsrc[4:8, :] = jnp.zeros((4, 128), jnp.int32)

    def tell(rel):
        return pltpu.make_async_remote_copy(
            src_ref=wsrc, dst_ref=wrecv.at[rel - 1], send_sem=wss.at[rel - 1], recv_sem=wrs.at[rel - 1],
            device_id={"tile": near(rel)}, device_id_type=MESH)

    def meta(side):
        return pltpu.make_async_remote_copy(
            src_ref=wsrc, dst_ref=mrecv.at[side], send_sem=mss.at[side], recv_sem=mrs.at[side],
            device_id={"tile": (right, left)[side]}, device_id_type=MESH)

    for rel in range(1, 4):
        tell(rel).start()
    meta(0).start()
    meta(1).start()

    loads[0].wait()
    loads[1].wait()

    def square_row(ref):
        part = jnp.zeros((cap, HEAD_DIM), F32)
        for c in range(heads):
            x = ref[:, c * HEAD_DIM : (c + 1) * HEAD_DIM].astype(F32)
            part = part + x * x
        return jnp.sum(part.T, axis=0, keepdims=True)

    ssrc[0:1, :] = square_row(qr)
    ssrc[1:2, :] = square_row(kr)
    sbuf[h] = ssrc[...]

    def share(i):
        return pltpu.make_async_remote_copy(
            src_ref=ssrc, dst_ref=sbuf.at[h], send_sem=sss.at[i - 1], recv_sem=srs.at[i - 1],
            device_id={"head": lax.rem(h + i, nh)}, device_id_type=MESH)

    def shared(i):
        return pltpu.make_async_remote_copy(
            src_ref=ssrc, dst_ref=sbuf.at[lax.rem(h + nh - i, nh)], send_sem=sss.at[i - 1], recv_sem=srs.at[i - 1],
            device_id={"head": lax.rem(h + i, nh)}, device_id_type=MESH)

    for i in range(1, nh):
        share(i).start()

    for i in range(heads):
        acc[i] = jnp.zeros((cap, HEAD_DIM), F32)
        mx[i] = jnp.full((cap, HEAD_DIM), NEG, F32)
        ls[i] = jnp.zeros((cap, HEAD_DIM), F32)

    @pl.when(t == 0)
    def _():
        ek[0:EDGE] = jnp.zeros((EDGE, wid), BF16)
        ev[0:EDGE] = jnp.zeros((EDGE, wid), BF16)

    @pl.when(t == tiles - 1)
    def _():
        ek[EDGE:] = jnp.zeros((EDGE, wid), BF16)
        ev[EDGE:] = jnp.zeros((EDGE, wid), BF16)

    to_smem = [pltpu.make_async_copy(wsrc, wsm.at[0], wls.at[0])]
    to_smem[0].start()
    for rel in range(1, 4):
        tell(rel).wait_recv()
        copy = pltpu.make_async_copy(wrecv.at[rel - 1], wsm.at[rel], wls.at[rel])
        copy.start()
        to_smem.append(copy)
    for copy in to_smem:
        copy.wait()

    def edge(side, x):
        src = ((tail_k, tail_v), (kn.at[pl.ds(0, EDGE)], vr.at[pl.ds(0, EDGE)]))[side][x]
        dst = (ek, ev)[x].at[pl.ds(side * EDGE, EDGE)]
        return pltpu.make_async_remote_copy(
            src_ref=src, dst_ref=dst, send_sem=ess.at[side, x], recv_sem=ers.at[side, x],
            device_id={"tile": (right, left)[side]}, device_id_type=MESH)

    def normalise():
        for i in range(1, nh):
            shared(i).wait_recv()
        total = sbuf[0]
        for i in range(1, nh):
            total = total + sbuf[i]
        factor = lax.rsqrt(total / width + EPSILON)
        for row, (raw, gain, out) in enumerate(((kr, gk_ref, kn), (qr, gq_ref, qn))):
            row = 1 - row
            wide = jnp.broadcast_to(factor[row : row + 1], (HEAD_DIM, cap)).T
            for c in range(heads):
                cols = slice(c * HEAD_DIM, (c + 1) * HEAD_DIM)
                out[:, cols] = (raw[:, cols].astype(F32) * wide * gain[:, cols]).astype(BF16)
        loads[4].wait()
        place = lax.broadcasted_iota(jnp.int32, (EDGE, cap), 0) + (length - EDGE)
        pick = (lax.broadcasted_iota(jnp.int32, (EDGE, cap), 1) == place).astype(F32).astype(BF16)
        tail_k[...] = jnp.dot(pick, kn[...], preferred_element_type=F32).astype(BF16)
        tail_v[...] = jnp.dot(pick, vr[...], preferred_element_type=F32).astype(BF16)

        @pl.when(t < tiles - 1)
        def _():
            for x in range(2):
                edge(0, x).start()

        @pl.when(t > 0)
        def _():
            for x in range(2):
                edge(1, x).start()

    def update(i, keys, values, bias):
        cols = pl.ds(pl.multiple_of(i * HEAD_DIM, HEAD_DIM), HEAD_DIM)
        scores = lax.dot_general(qn[:, cols], keys(cols), (((1,), (1,)), ((), ())), preferred_element_type=F32)
        scores = scores * SCORE_SCALE + bias
        before = mx[i]
        now = jnp.maximum(before, jnp.max(scores, axis=1, keepdims=True))
        expo = jnp.exp2(scores - now[:, :1])
        keep = jnp.exp2(before - now)
        mx[i] = now
        ls[i] = ls[i] * keep + jnp.sum(expo, axis=1, keepdims=True)
        acc[i] = acc[i] * keep + jnp.dot(expo.astype(BF16), values(cols), preferred_element_type=F32)

    def own_attention(i):
        spot = lax.broadcasted_iota(jnp.int32, (1, cap), 1)
        ok_own = jnp.where(spot < length, 0.0, NEG).astype(F32)
        slot = lax.broadcasted_iota(jnp.int32, (1, 2 * EDGE), 1)
        ll, lsess = mrecv[0, 2:3, :], mrecv[0, 3:4, :]
        rl, rsess = mrecv[1, 2:3, :], mrecv[1, 3:4, :]
        from_left = (slot < EDGE) & (lsess == jnp.where(t > 0, session, -1)) & (slot >= EDGE - ll)
        from_right = (slot >= EDGE) & (rsess == jnp.where(t < tiles - 1, session, -1)) & (slot - EDGE < rl)
        ok_edge = jnp.where(from_left | from_right, 0.0, NEG).astype(F32)
        update(
            i,
            lambda c: jnp.concatenate([kn[:, c], ek[:, c]], 0),
            lambda c: jnp.concatenate([vr[:, c], ev[:, c]], 0),
            jnp.concatenate([ok_own, ok_edge], 1),
        )

    def origin(r):
        return lax.rem(z + nz - r, nz)

    def pick_out(r, src_k, src_v):
        owner = origin(r) * 4 + sub
        for rel in range(4):
            for slot in range(2):
                want = jnp.maximum(wsm[rel, slot, owner], 0)
                if rel == 0:
                    mkk[r, slot] = src_k[want]
                    mvv[r, slot] = src_v[want]
                else:
                    selk[rel - 1, r, slot] = src_k[want]
                    selv[rel - 1, r, slot] = src_v[want]

    def give(rel, r, x):
        src, dst = ((selk, mkk), (selv, mvv))[x]
        return pltpu.make_async_remote_copy(
            src_ref=src.at[rel - 1, r], dst_ref=dst.at[r, pl.ds(2 * rel, 2)],
            send_sem=pss.at[rel - 1, r, x], recv_sem=prs.at[rel - 1, r, x],
            device_id={"tile": near(rel)}, device_id_type=MESH)

    def hand_out(r, src_k, src_v):
        pick_out(r, src_k, src_v)
        for rel in (2, 3, 1):
            for x in range(2):
                give(rel, r, x).start()

    def chunk(ra, rb):
        for r in (ra, rb):
            for rel in range(1, 4):
                for x in range(2):
                    give(rel, r, x).wait_recv()
        group = lane // 8
        bias = jnp.zeros((1, 128), F32)
        for j, r in enumerate((ra, rb)):
            for rel in range(4):
                for slot in range(2):
                    want = wsm[0, slot, origin(r) * 4 + near(rel) - z * 4]
                    miss = jnp.where(want < 0, NEG, 0.0).astype(F32)
                    bias = jnp.where(group == j * 8 + rel * 2 + slot, miss, bias)

        def rows(ref, c):
            return jnp.concatenate([ref[r, :, :, c].reshape(64, HEAD_DIM) for r in (ra, rb)], 0)

        @pl.loop(0, heads)
        def _(i):
            update(i, lambda c: rows(mkk, c), lambda c: rows(mvv, c), bias)

    loads[2].wait()
    loads[3].wait()
    cur_ka[...] = kb[0]
    cur_va[...] = vb[0]
    hand_out(0, cur_ka, cur_va)

    def arrived(s, x, last):
        for d in range(2):
            hop(d, s, x).wait_recv()
            if not last or d == x:
                hop(d, s + 1, x).start()

    def take(s):
        cur_ka[...] = kb[s]
        cur_va[...] = vb[s]
        cur_kb[...] = kb[nz - s]
        cur_vb[...] = vb[nz - s]
        hand_out(s, cur_ka, cur_va)
        hand_out(nz - s, cur_kb, cur_vb)

    arrived(1, 0, half == 2)
    normalise()
    arrived(1, 1, half == 2)
    take(1)
    meta(0).wait_recv()
    meta(1).wait_recv()
    for side, there in ((0, t > 0), (1, t < tiles - 1)):

        @pl.when(there)
        def _(side=side):
            for x in range(2):
                edge(side, x).wait_recv()

    @pl.loop(2, half - 1)
    def _(s):
        arrived(s, 0, False)
        pl.when(s - 2 < heads)(lambda: own_attention(s - 2))
        arrived(s, 1, False)
        take(s)
        chunk(s - 1, nz - s + 1)

    if half > 2:
        arrived(half - 1, 0, True)
        arrived(half - 1, 1, True)
        take(half - 1)
        chunk(half - 2, nz - half + 2)
    for i in range(max(0, half - 3), heads):
        own_attention(i)
    hop(0, half, 0).wait_recv()
    cur_ka[...] = kb[half]
    hop(1, half, 1).wait_recv()
    cur_va[...] = vb[half]
    hand_out(half, cur_ka, cur_va)
    chunk(half - 1, nz - half + 1)
    chunk(0, half)

    live = lax.broadcasted_iota(jnp.int32, (cap, HEAD_DIM), 0) < length
    for i in range(heads):
        out = jnp.where(live, acc[i] / ls[i], 0.0)
        o_ref[:, i * HEAD_DIM : (i + 1) * HEAD_DIM] = out.astype(BF16)

    for s in range(1, half + 1):
        for x in range(2):
            for d in range(2):
                if s < half or d == x:
                    hop(d, s, x).wait_send()
    for rel in range(1, 4):
        tell(rel).wait_send()
        for r in range(nz):
            for x in range(2):
                give(rel, r, x).wait_send()
    for i in range(1, nh):
        share(i).wait_send()
    for side, there in ((0, t < tiles - 1), (1, t > 0)):
        meta(side).wait_send()

        @pl.when(there)
        def _(side=side):
            for x in range(2):
                edge(side, x).wait_send()


def per_device(tiles, nh, width, q, k, v, gq, gk, mk, mv, tile_len, session, owner, index):
    nz, half = tiles // 4, tiles // 8
    (cap, wid), (blocks, rows, _) = q.shape, mk.shape
    heads = wid // HEAD_DIM
    smem = pl.BlockSpec(memory_space=pltpu.SMEM)
    vmem = pl.BlockSpec(memory_space=pltpu.VMEM)
    any_space = pl.BlockSpec(memory_space=pl.ANY)
    sem = pltpu.SemaphoreType.DMA
    tile = pltpu.VMEM((cap, wid), BF16)
    state = pltpu.VMEM((heads, cap, HEAD_DIM), F32)
    block = pltpu.VMEM((blocks, rows, wid), BF16)
    edge = pltpu.VMEM((EDGE, wid), BF16)
    return pl.pallas_call(
        functools.partial(kernel, tiles, nh, width),
        out_shape=jax.ShapeDtypeStruct((cap, wid), BF16),
        in_specs=[smem] * 4 + [vmem] * 2 + [any_space] * 5,
        out_specs=vmem,
        scratch_shapes=[
            pltpu.VMEM((nz, blocks, rows, wid), BF16),
            pltpu.VMEM((nz, blocks, rows, wid), BF16),
            block, block, block, block,
            tile, tile, tile, tile, tile,
            pltpu.VMEM((2, cap), F32),
            pltpu.VMEM((nh, 2, cap), F32),
            pltpu.VMEM((8, 128), jnp.int32),
            pltpu.VMEM((3, 8, 128), jnp.int32),
            pltpu.VMEM((2, 8, 128), jnp.int32),
            pltpu.SMEM((4, 8, 128), jnp.int32),
            edge, edge,
            pltpu.VMEM((2 * EDGE, wid), BF16),
            pltpu.VMEM((2 * EDGE, wid), BF16),
            pltpu.VMEM((3, nz, 2, rows, wid), BF16),
            pltpu.VMEM((3, nz, 2, rows, wid), BF16),
            pltpu.VMEM((nz, 8, rows, wid), BF16),
            pltpu.VMEM((nz, 8, rows, wid), BF16),
            state, state, state,
            sem((2, half, 2)), sem((2, half, 2)), sem((5,)),
            sem((max(1, nh - 1),)), sem((max(1, nh - 1),)),
            sem((3,)), sem((3,)), sem((4,)),
            sem((2,)), sem((2,)), sem((2, 2)), sem((2, 2)),
            sem((3, nz, 2)), sem((3, nz, 2)),
        ],
        compiler_params=pltpu.CompilerParams(
            collective_id=0, has_side_effects=True, vmem_limit_bytes=60 * 1024 * 1024
        ),
        name="tile_attention",
    )(
        tile_len, session, owner.reshape(-1), index, gq.reshape(1, -1), gk.reshape(1, -1),
        q, k, v, mk, mv,
    )


def solution(mesh):
    in_specs = (
        P("tile", "head"),
        P("tile", "head"),
        P("tile", "head"),
        P("head"),
        P("head"),
        P("tile", None, "head"),
        P("tile", None, "head"),
        P("tile"),
        P("tile"),
        P("tile", None),
        P("tile"),
    )
    tiles, nh = mesh.shape["tile"], mesh.shape["head"]

    def whole(q, *rest):
        body = functools.partial(per_device, tiles, nh, q.shape[1])
        return jax.shard_map(
            body, mesh=mesh, in_specs=in_specs, out_specs=P("tile", "head"), check_vma=False
        )(q, *rest)

    return whole
```

```python
import functools
import math

import jax
import jax.numpy as jnp
from jax import lax
from jax.experimental import pallas as pl
from jax.experimental.pallas import tpu as pltpu
from jax.sharding import PartitionSpec as P

HEAD_DIM = 128
EDGE = 64
EPSILON = 1e-06
MESH = pl.DeviceIdType.MESH
NEG = -1e30
BF16 = jnp.bfloat16
F32 = jnp.float32
SCORE_SCALE = (1.0 / HEAD_DIM**0.5) * math.log2(math.e)


def kernel(
    tiles, nh, width,
    msrc, own_ref, idx_ref, gq_hbm, gk_hbm,
    q_hbm, k_hbm, v_hbm, mk_hbm, mv_hbm, o_ref,
    kvb, cur_ka, cur_va, cur_kb, cur_vb,
    qr, kr, vr, qn, kn,
    gq_ref, gk_ref,
    ssrc, sbuf, shalf, sother, wsrc, wnear, wfar, mrecv, snear, sfar,
    tail, ekv, sel, far, mkk, mvv,
    acc, mx, ls,
    out_sem, hop_sem, loc, table_sem, near_sem, edge_out, edge_in, tab_loc,
):
    nz, half = tiles // 4, tiles // 8
    full = half - 2
    cap, wid = qr.shape
    heads = wid // HEAD_DIM
    t, h = lax.axis_index("tile"), lax.axis_index("head")
    z, sub = t // 4, lax.rem(t, 4)
    up, dn = lax.rem(t + 4, tiles), lax.rem(t + tiles - 4, tiles)
    right, left = lax.rem(t + 1, tiles), lax.rem(t + tiles - 1, tiles)

    def near(rel):
        other = sub + jnp.where(lax.rem(sub, 2) == 0, 1, -1) * (rel % 2)
        other = other + jnp.where(sub // 2 == 0, 2, -2) * (rel // 2)
        return z * 4 + other

    def landed(ref, semaphore):
        pltpu.make_async_copy(ref, ref, semaphore).wait()

    bar = pltpu.get_barrier_semaphore()
    steps = (1, -1, 2, -2)

    def at(dz, rel):
        return lax.rem(z + dz + nz, nz) * 4 + near(rel) - z * 4

    greet = [{"tile": near(rel)} for rel in range(1, 4)]
    greet += [{"tile": at(dz, rel)} for dz in steps for rel in range(4)]
    greet += [{"head": lax.rem(h + 2 * i, nh)} for i in range(1, nh // 2)]
    hpair = h + jnp.where(lax.rem(h, 2) == 0, 1, -1)
    greet += [{"head": hpair}]
    for n in greet:
        pl.semaphore_signal(bar, inc=1, device_id=n, device_id_type=MESH)
    pl.semaphore_wait(bar, len(greet))

    def hop(d, s, x):
        first = (mk_hbm, mv_hbm)[x]
        static = isinstance(s, int)
        if d == 0:
            src, dst, dev = s - 1, s, up
        else:
            src, dst, dev = nz + 1 - s, nz - s, dn
        return pltpu.make_async_remote_copy(
            src_ref=first if static and s == 1 else kvb.at[x * nz + src], dst_ref=kvb.at[x * nz + dst],
            send_sem=out_sem.at[0], recv_sem=hop_sem.at[d, s - 1, x],
            device_id={"tile": dev}, device_id_type=MESH)

    for x in range(2):
        for d in range(2):
            hop(d, 1, x).start()

    loads = [
        pltpu.make_async_copy(a, b, loc.at[i])
        for i, (a, b) in enumerate((
            (q_hbm, qr), (k_hbm, kr), (mk_hbm, kvb.at[0]), (mv_hbm, kvb.at[nz]), (v_hbm, vr),
            (gq_hbm, gq_ref), (gk_hbm, gk_ref),
        ))
    ]
    for copy in loads:
        copy.start()

    lane = lax.broadcasted_iota(jnp.int32, (1, 128), 1)

    def ask(r, carry):
        w0, w1 = carry
        hit, b = lane == own_ref[r], idx_ref[r]
        return (
            jnp.where(jnp.logical_and(hit, w0 < 0), b, w0),
            jnp.where(jnp.logical_and(hit, w0 >= 0), b, w1),
        )

    none = jnp.full((1, 128), -1, jnp.int32)
    w0, w1 = lax.fori_loop(0, own_ref.shape[0], ask, (none, none))
    length, session = msrc[0:1, 0:1], msrc[1:2, 0:1]
    wsrc[0:1, :] = w0
    wsrc[1:2, :] = w1

    def tell(rel):
        return pltpu.make_async_remote_copy(
            src_ref=wsrc, dst_ref=wnear.at[rel], send_sem=out_sem.at[1], recv_sem=table_sem.at[0],
            device_id={"tile": near(rel)}, device_id_type=MESH)

    def tell_far(i, rel):
        return pltpu.make_async_remote_copy(
            src_ref=wsrc, dst_ref=wfar.at[(i ^ 1) * 4 + rel], send_sem=out_sem.at[2], recv_sem=table_sem.at[1],
            device_id={"tile": at(steps[i], rel)}, device_id_type=MESH)

    def meta(side):
        return pltpu.make_async_remote_copy(
            src_ref=msrc, dst_ref=mrecv.at[side], send_sem=out_sem.at[3], recv_sem=table_sem.at[2],
            device_id={"tile": (right, left)[side]}, device_id_type=MESH)

    wnear[0] = wsrc[...]
    for rel in range(1, 4):
        tell(rel).start()
    meta(0).start()
    meta(1).start()
    for i in range(4):
        for rel in range(4):
            tell_far(i, rel).start()

    loads[0].wait()
    loads[1].wait()

    def square_row(ref):
        part = jnp.zeros((cap, HEAD_DIM), F32)
        for c in range(heads):
            x = ref[:, c * HEAD_DIM : (c + 1) * HEAD_DIM].astype(F32)
            part = part + x * x
        return jnp.sum(part.T, axis=0, keepdims=True)

    ssrc[0:1, :] = square_row(qr)
    ssrc[1:2, :] = square_row(kr)
    sbuf[h // 2] = ssrc[...]

    def share(i):
        return pltpu.make_async_remote_copy(
            src_ref=ssrc, dst_ref=sbuf.at[h // 2], send_sem=out_sem.at[4], recv_sem=table_sem.at[3],
            device_id={"head": lax.rem(h + 2 * i, nh)}, device_id_type=MESH)

    for i in range(1, nh // 2):
        share(i).start()

    pair = pltpu.make_async_remote_copy(
        src_ref=shalf, dst_ref=sother, send_sem=out_sem.at[5], recv_sem=table_sem.at[4],
        device_id={"head": hpair}, device_id_type=MESH)

    for i in range(heads):
        acc[i] = jnp.zeros((cap, HEAD_DIM), F32)
        mx[i] = jnp.full((cap, HEAD_DIM), NEG, F32)
        ls[i] = jnp.zeros((cap, HEAD_DIM), F32)

    @pl.when(t == 0)
    def _():
        ekv[0] = jnp.zeros((2, EDGE, wid), BF16)

    @pl.when(t == tiles - 1)
    def _():
        ekv[1] = jnp.zeros((2, EDGE, wid), BF16)

    landed(wnear.at[pl.ds(1, 3)], table_sem.at[0])
    copy = pltpu.make_async_copy(wnear, snear, tab_loc.at[0])
    copy.start()
    copy.wait()

    def edge(side, x):
        src = (tail.at[x], (kn, vr)[x].at[pl.ds(0, EDGE)])[side]
        return pltpu.make_async_remote_copy(
            src_ref=src, dst_ref=ekv.at[side, x], send_sem=edge_out.at[side], recv_sem=edge_in.at[side],
            device_id={"tile": (right, left)[side]}, device_id_type=MESH)

    def normalise():
        pair.wait_recv()
        loads[5].wait()
        loads[6].wait()
        factor = lax.rsqrt((shalf[...] + sother[...]) / width + EPSILON)
        for row, (raw, gain, out) in enumerate(((kr, gk_ref, kn), (qr, gq_ref, qn))):
            row = 1 - row
            wide = jnp.broadcast_to(factor[row : row + 1], (HEAD_DIM, cap)).T
            for c in range(heads):
                cols = slice(c * HEAD_DIM, (c + 1) * HEAD_DIM)
                out[:, cols] = (raw[:, cols].astype(F32) * wide * gain[cols].reshape(1, HEAD_DIM)).astype(BF16)
        loads[4].wait()
        place = lax.broadcasted_iota(jnp.int32, (EDGE, cap), 0) + (length - EDGE)
        pick = (lax.broadcasted_iota(jnp.int32, (EDGE, cap), 1) == place).astype(F32).astype(BF16)
        tail[0] = jnp.dot(pick, kn[...], preferred_element_type=F32).astype(BF16)
        tail[1] = jnp.dot(pick, vr[...], preferred_element_type=F32).astype(BF16)

        @pl.when(t < tiles - 1)
        def _():
            for x in range(2):
                edge(0, x).start()

        @pl.when(t > 0)
        def _():
            for x in range(2):
                edge(1, x).start()

    def update(i, keys, values, bias):
        cols = pl.ds(pl.multiple_of(i * HEAD_DIM, HEAD_DIM), HEAD_DIM)
        scores = lax.dot_general(qn[:, cols], keys(cols), (((1,), (1,)), ((), ())), preferred_element_type=F32)
        scores = scores * SCORE_SCALE + bias
        before = mx[i]
        now = jnp.maximum(before, jnp.max(scores, axis=1, keepdims=True))
        expo = jnp.exp2(scores - now[:, :1])
        keep = jnp.exp2(before - now)
        mx[i] = now
        ls[i] = ls[i] * keep + jnp.sum(expo, axis=1, keepdims=True)
        acc[i] = acc[i] * keep + jnp.dot(expo.astype(BF16), values(cols), preferred_element_type=F32)

    def own_attention(i):
        spot = lax.broadcasted_iota(jnp.int32, (1, cap), 1)
        ok_own = jnp.where(spot < length, 0.0, NEG).astype(F32)
        slot = lax.broadcasted_iota(jnp.int32, (1, 2 * EDGE), 1)
        ll, lsess = mrecv[0, 0:1, :], mrecv[0, 1:2, :]
        rl, rsess = mrecv[1, 0:1, :], mrecv[1, 1:2, :]
        from_left = (slot < EDGE) & (lsess == jnp.where(t > 0, session, -1)) & (slot >= EDGE - ll)
        from_right = (slot >= EDGE) & (rsess == jnp.where(t < tiles - 1, session, -1)) & (slot - EDGE < rl)
        ok_edge = jnp.where(from_left | from_right, 0.0, NEG).astype(F32)
        update(
            i,
            lambda c: jnp.concatenate([kn[:, c], ekv[0, 0, :, c], ekv[1, 0, :, c]], 0),
            lambda c: jnp.concatenate([vr[:, c], ekv[0, 1, :, c], ekv[1, 1, :, c]], 0),
            jnp.concatenate([ok_own, ok_edge], 1),
        )

    def origin(r):
        return lax.rem(z + nz - r, nz)

    def hand_out(r, x, src):
        owner = origin(r) * 4 + sub
        for rel in (2, 3, 1, 0):
            out = (mkk, mvv)[x].at[r, pl.ds(0, 2)] if rel == 0 else sel.at[(x * 3 + rel - 1) * nz + r]
            for slot in range(2):
                out[slot] = src[jnp.maximum(snear[rel, slot, owner], 0)]
            if rel > 0:
                pltpu.make_async_remote_copy(
                    src_ref=sel.at[(x * 3 + rel - 1) * nz + r], dst_ref=(mkk, mvv)[x].at[r, pl.ds(2 * rel, 2)],
                    send_sem=out_sem.at[6], recv_sem=near_sem.at[r],
                    device_id={"tile": near(rel)}, device_id_type=MESH).start()

    def far_out(d, x, src):
        owner = origin(full if d == 0 else nz - full) * 4 + sub
        for far_by in (1, 2) if d == x else (1,):
            i, r = (far_by - 1) * 2 + d, (full + far_by) if d == 0 else nz - full - far_by
            for rel in range(4):
                place = (d * 2 + x if far_by == 1 else 4 + d) * 4 + rel
                for slot in range(2):
                    far[place, slot] = src[jnp.maximum(sfar[i * 4 + rel, slot, owner], 0)]
                pltpu.make_async_remote_copy(
                    src_ref=far.at[place], dst_ref=(mkk, mvv)[x].at[r, pl.ds(2 * rel, 2)],
                    send_sem=out_sem.at[7], recv_sem=near_sem.at[r],
                    device_id={"tile": at(steps[i], rel)}, device_id_type=MESH).start()

    def chunk(slots, beyond, loop):
        for r in slots:
            away = beyond and isinstance(r, int) and full < r < nz - full
            landed(sel.at[pl.ds(0, 8 if away else 6)], near_sem.at[r])
        group = lane // 8
        biases = []
        for pair_of in (slots[i : i + 2] for i in range(0, len(slots), 2)):
            bias = jnp.full((1, 128), NEG, F32)
            for j, r in enumerate(pair_of):
                for rel in range(4):
                    for slot in range(2):
                        want = snear[0, slot, origin(r) * 4 + near(rel) - z * 4]
                        miss = jnp.where(want < 0, NEG, 0.0).astype(F32)
                        bias = jnp.where(group == j * 8 + rel * 2 + slot, miss, bias)
            biases.append(bias[:, : 64 * len(pair_of)])
        bias = biases[0] if len(biases) == 1 else jnp.concatenate(biases, 1)

        def rows(ref, c):
            return jnp.concatenate([ref[r, :, :, c].reshape(64, HEAD_DIM) for r in slots], 0)

        def one(i):
            update(i, lambda c: rows(mkk, c), lambda c: rows(mvv, c), bias)

        if loop:
            pl.loop(0, heads)(one)
        else:
            for i in range(heads):
                one(i)

    loads[2].wait()
    loads[3].wait()
    cur_ka[...] = kvb[0]
    cur_va[...] = kvb[nz]
    hand_out(0, 0, cur_ka)
    hand_out(0, 1, cur_va)

    def arrived(s, x):
        for d in range(2):
            hop(d, s, x).wait_recv()
            hop(d, s + 1, x).start()

    def take(s, x):
        up_cur, dn_cur = ((cur_ka, cur_kb), (cur_va, cur_vb))[x]
        up_cur[...] = kvb[x * nz + s]
        dn_cur[...] = kvb[x * nz + nz - s]
        hand_out(s, x, up_cur)
        hand_out(nz - s, x, dn_cur)

    def halves():
        landed(sbuf.at[pl.ds(0, nh // 2 - 1)], table_sem.at[3])
        total = sbuf[0]
        for i in range(1, nh // 2):
            total = total + sbuf[i]
        shalf[...] = total
        pair.start()

    arrived(1, 0)
    take(1, 0)
    halves()
    arrived(1, 1)
    take(1, 1)
    normalise()
    arrived(2, 0)
    take(2, 0)
    arrived(2, 1)
    take(2, 1)
    chunk((1, nz - 1), False, True)
    landed(mrecv, table_sem.at[2])
    for side, there in ((0, t > 0), (1, t < tiles - 1)):

        @pl.when(there)
        def _(side=side):
            landed(ekv.at[side], edge_in.at[side])

    @pl.loop(3, full)
    def _(s):
        arrived(s, 0)
        take(s, 0)
        pl.when(s - 3 < heads)(lambda: own_attention(s - 3))
        arrived(s, 1)
        take(s, 1)
        chunk((s - 1, nz - s + 1), False, True)

    landed(wfar, table_sem.at[1])
    copy = pltpu.make_async_copy(wfar, sfar, tab_loc.at[1])
    copy.start()
    copy.wait()
    for x, (up_cur, dn_cur) in enumerate(((cur_ka, cur_kb), (cur_va, cur_vb))):
        hop(0, full, x).wait_recv()
        hop(1, full, x).wait_recv()
        take(full, x)
        far_out(0, x, up_cur)
        far_out(1, x, dn_cur)
    chunk((full - 1, nz - full + 1), False, True)
    for i in range(max(0, full - 3), heads):
        own_attention(i)
    chunk((0,), False, True)
    chunk((full, nz - full, half - 1, nz - half + 1, half), True, False)
    for i in range(heads):
        o_ref[:, i * HEAD_DIM : (i + 1) * HEAD_DIM] = (acc[i] / ls[i]).astype(BF16)

    landed(kvb.at[pl.ds(0, 4 * full)], out_sem.at[0])
    landed(wnear.at[pl.ds(0, 3)], out_sem.at[1])
    landed(wfar, out_sem.at[2])
    landed(mrecv, out_sem.at[3])
    landed(sbuf.at[pl.ds(0, nh // 2 - 1)], out_sem.at[4])
    pair.wait_send()
    landed(sel.at[pl.ds(0, 6 * (2 * full + 1))], out_sem.at[6])
    landed(far, out_sem.at[7])
    for side, there in ((0, t < tiles - 1), (1, t > 0)):

        @pl.when(there)
        def _(side=side):
            landed(ekv.at[side], edge_out.at[side])


def per_device(tiles, nh, width, q, k, v, gq, gk, mk, mv, tile_len, session, owner, index):
    nz, half = tiles // 4, tiles // 8
    (cap, wid), (blocks, rows, _) = q.shape, mk.shape
    heads = wid // HEAD_DIM
    smem = pl.BlockSpec(memory_space=pltpu.SMEM)
    vmem = pl.BlockSpec(memory_space=pltpu.VMEM)
    hbm = pl.BlockSpec(memory_space=pltpu.HBM)
    sem = pltpu.SemaphoreType.DMA
    tile = pltpu.VMEM((cap, wid), BF16)
    state = pltpu.VMEM((heads, cap, HEAD_DIM), F32)
    block = pltpu.VMEM((blocks, rows, wid), BF16)
    meta = jnp.where(lax.broadcasted_iota(jnp.int32, (2, 128), 0) == 0, tile_len[0], session[0])
    attended = pl.pallas_call(
        functools.partial(kernel, tiles, nh, width),
        out_shape=jax.ShapeDtypeStruct((cap, wid), BF16),
        in_specs=[vmem] + [smem] * 2 + [hbm] * 7,
        out_specs=vmem,
        scratch_shapes=[
            pltpu.VMEM((2 * nz, blocks, rows, wid), BF16),
            block, block, block, block,
            tile, tile, tile, tile, tile,
            pltpu.VMEM((wid,), F32),
            pltpu.VMEM((wid,), F32),
            pltpu.VMEM((2, cap), F32),
            pltpu.VMEM((nh // 2, 2, cap), F32),
            pltpu.VMEM((2, cap), F32),
            pltpu.VMEM((2, cap), F32),
            pltpu.VMEM((2, 128), jnp.int32),
            pltpu.VMEM((4, 2, 128), jnp.int32),
            pltpu.VMEM((16, 2, 128), jnp.int32),
            pltpu.VMEM((2, 2, 128), jnp.int32),
            pltpu.SMEM((4, 2, 128), jnp.int32),
            pltpu.SMEM((16, 2, 128), jnp.int32),
            pltpu.VMEM((2, EDGE, wid), BF16),
            pltpu.VMEM((2, 2, EDGE, wid), BF16),
            pltpu.VMEM((6 * nz, 2, rows, wid), BF16),
            pltpu.VMEM((24, 2, rows, wid), BF16),
            pltpu.VMEM((nz, 8, rows, wid), BF16),
            pltpu.VMEM((nz, 8, rows, wid), BF16),
            state, state, state,
            sem((8,)), sem((2, half - 2, 2)), sem((7,)), sem((5,)), sem((nz,)), sem((2,)), sem((2,)), sem((2,)),
        ],
        compiler_params=pltpu.CompilerParams(
            collective_id=0, has_side_effects=True, vmem_limit_bytes=60 * 1024 * 1024
        ),
        name="tile_attention",
    )(
        meta, owner.reshape(-1), index, gq, gk, q, k, v, mk, mv,
    )
    live = lax.broadcasted_iota(jnp.int32, (cap, wid), 0) < tile_len[0]
    return jnp.where(live, attended, jnp.bfloat16(0))


def solution(mesh):
    in_specs = (
        P("tile", "head"),
        P("tile", "head"),
        P("tile", "head"),
        P("head"),
        P("head"),
        P("tile", None, "head"),
        P("tile", None, "head"),
        P("tile"),
        P("tile"),
        P("tile", None),
        P("tile"),
    )
    tiles, nh = mesh.shape["tile"], mesh.shape["head"]

    def whole(q, *rest):
        body = functools.partial(per_device, tiles, nh, q.shape[1])
        return jax.shard_map(
            body, mesh=mesh, in_specs=in_specs, out_specs=P("tile", "head"), check_vma=False
        )(q, *rest)

    return whole
```

```python
import functools
import math

import jax
import jax.numpy as jnp
from jax import lax
from jax.experimental import pallas as pl
from jax.experimental.pallas import tpu as pltpu
from jax.sharding import PartitionSpec as P

HEAD_DIM = 128
EDGE = 64
EPSILON = 1e-06
MESH = pl.DeviceIdType.MESH
NEG = -1e30
BF16 = jnp.bfloat16
F32 = jnp.float32
SCORE_SCALE = (1.0 / HEAD_DIM**0.5) * math.log2(math.e)


def kernel(
    tiles, nh, width,
    len_ref, ses_ref, own_hbm, idx_hbm, gq_hbm, gk_hbm,
    q_hbm, k_hbm, v_hbm, mk_hbm, mv_hbm, o_ref,
    kvb, cur_ka, cur_va, cur_kb, cur_vb,
    qr, kr, vr, qn, kn,
    gq_ref, gk_ref, own_ref, idx_ref,
    ssrc, sbuf, shalf, sother, wnear, wfar, msrc, mrecv, snear, sfar,
    tail, ekv, sel, far, mkk, mvv,
    acc, mx, ls,
    out_sem, hop_sem, loc, table_sem, near_sem, edge_out, edge_in, tab_loc,
):
    nz, half = tiles // 4, tiles // 8
    full = half - 2
    cap, wid = qr.shape
    heads = wid // HEAD_DIM
    t, h = lax.axis_index("tile"), lax.axis_index("head")
    z, sub = t // 4, lax.rem(t, 4)
    up, dn = lax.rem(t + 4, tiles), lax.rem(t + tiles - 4, tiles)
    right, left = lax.rem(t + 1, tiles), lax.rem(t + tiles - 1, tiles)

    def near(rel):
        other = sub + jnp.where(lax.rem(sub, 2) == 0, 1, -1) * (rel % 2)
        other = other + jnp.where(sub // 2 == 0, 2, -2) * (rel // 2)
        return z * 4 + other

    def landed(ref, semaphore):
        pltpu.make_async_copy(ref, ref, semaphore).wait()

    bar = pltpu.get_barrier_semaphore()
    steps = (1, -1, 2, -2)

    def at(dz, rel):
        return lax.rem(z + dz + nz, nz) * 4 + near(rel) - z * 4

    greet = [{"tile": near(rel)} for rel in range(1, 4)]
    greet += [{"tile": at(dz, rel)} for dz in steps for rel in range(4)]
    greet += [{"head": lax.rem(h + 2 * i, nh)} for i in range(1, nh // 2)]
    hpair = h + jnp.where(lax.rem(h, 2) == 0, 1, -1)
    greet += [{"head": hpair}]
    for n in greet:
        pl.semaphore_signal(bar, inc=1, device_id=n, device_id_type=MESH)
    pl.semaphore_wait(bar, len(greet))

    def hop(d, s, x):
        first = (mk_hbm, mv_hbm)[x]
        static = isinstance(s, int)
        if d == 0:
            src, dst, dev = s - 1, s, up
        else:
            src, dst, dev = nz + 1 - s, nz - s, dn
        return pltpu.make_async_remote_copy(
            src_ref=first if static and s == 1 else kvb.at[x * nz + src], dst_ref=kvb.at[x * nz + dst],
            send_sem=out_sem.at[0], recv_sem=hop_sem.at[d, s - 1, x],
            device_id={"tile": dev}, device_id_type=MESH)

    for x in range(2):
        for d in range(2):
            hop(d, 1, x).start()

    loads = [
        pltpu.make_async_copy(a, b, loc.at[i])
        for i, (a, b) in enumerate((
            (q_hbm, qr), (k_hbm, kr), (mk_hbm, kvb.at[0]), (mv_hbm, kvb.at[nz]), (v_hbm, vr),
            (gq_hbm, gq_ref), (gk_hbm, gk_ref), (own_hbm, own_ref), (idx_hbm, idx_ref),
        ))
    ]
    for i in (7, 8, 0, 1, 2, 3, 4, 5, 6):
        loads[i].start()

    lane = lax.broadcasted_iota(jnp.int32, (1, 128), 1)

    def ask(r, carry):
        w0, w1 = carry
        hit, b = lane == own_ref[r], idx_ref[r]
        return (
            jnp.where(jnp.logical_and(hit, w0 < 0), b, w0),
            jnp.where(jnp.logical_and(hit, w0 >= 0), b, w1),
        )

    none = jnp.full((1, 128), -1, jnp.int32)
    loads[7].wait()
    loads[8].wait()
    w0, w1 = lax.fori_loop(0, own_ref.shape[0], ask, (none, none))
    length, session = len_ref[0], ses_ref[0]
    wnear[0, 0:1, :] = w0
    wnear[0, 1:2, :] = w1
    msrc[0:1, :] = jnp.full((1, 128), length, jnp.int32)
    msrc[1:2, :] = jnp.full((1, 128), session, jnp.int32)

    def tell(rel):
        return pltpu.make_async_remote_copy(
            src_ref=wnear.at[0], dst_ref=wnear.at[rel], send_sem=out_sem.at[1], recv_sem=table_sem.at[0],
            device_id={"tile": near(rel)}, device_id_type=MESH)

    def tell_far(i):
        return pltpu.make_async_remote_copy(
            src_ref=wnear, dst_ref=wfar.at[pl.ds((i ^ 1) * 4, 4)], send_sem=out_sem.at[2], recv_sem=table_sem.at[1],
            device_id={"tile": at(steps[i], 0)}, device_id_type=MESH)

    def meta(side):
        return pltpu.make_async_remote_copy(
            src_ref=msrc, dst_ref=mrecv.at[side], send_sem=out_sem.at[3], recv_sem=table_sem.at[2],
            device_id={"tile": (right, left)[side]}, device_id_type=MESH)

    for rel in range(1, 4):
        tell(rel).start()
    meta(0).start()
    meta(1).start()

    loads[0].wait()
    loads[1].wait()

    def square_row(ref):
        part = jnp.zeros((cap, HEAD_DIM), F32)
        for c in range(heads):
            x = ref[:, c * HEAD_DIM : (c + 1) * HEAD_DIM].astype(F32)
            part = part + x * x
        return jnp.sum(part.T, axis=0, keepdims=True)

    ssrc[0:1, :] = square_row(qr)
    ssrc[1:2, :] = square_row(kr)
    sbuf[h // 2] = ssrc[...]

    def share(i):
        return pltpu.make_async_remote_copy(
            src_ref=ssrc, dst_ref=sbuf.at[h // 2], send_sem=out_sem.at[4], recv_sem=table_sem.at[3],
            device_id={"head": lax.rem(h + 2 * i, nh)}, device_id_type=MESH)

    for i in range(1, nh // 2):
        share(i).start()

    pair = pltpu.make_async_remote_copy(
        src_ref=shalf, dst_ref=sother, send_sem=out_sem.at[5], recv_sem=table_sem.at[4],
        device_id={"head": hpair}, device_id_type=MESH)

    for i in range(heads):
        acc[i] = jnp.zeros((cap, HEAD_DIM), F32)
        mx[i] = jnp.full((cap, HEAD_DIM), NEG, F32)
        ls[i] = jnp.zeros((cap, HEAD_DIM), F32)

    @pl.when(t == 0)
    def _():
        ekv[0] = jnp.zeros((2, EDGE, wid), BF16)

    @pl.when(t == tiles - 1)
    def _():
        ekv[1] = jnp.zeros((2, EDGE, wid), BF16)

    landed(wnear.at[pl.ds(1, 3)], table_sem.at[0])
    copy = pltpu.make_async_copy(wnear, snear, tab_loc.at[0])
    copy.start()
    for i in range(4):
        tell_far(i).start()
    copy.wait()

    def edge(side, x):
        src = (tail.at[x], (kn, vr)[x].at[pl.ds(0, EDGE)])[side]
        return pltpu.make_async_remote_copy(
            src_ref=src, dst_ref=ekv.at[side, x], send_sem=edge_out.at[side], recv_sem=edge_in.at[side],
            device_id={"tile": (right, left)[side]}, device_id_type=MESH)

    def normalise():
        pair.wait_recv()
        loads[5].wait()
        loads[6].wait()
        factor = lax.rsqrt((shalf[...] + sother[...]) / width + EPSILON)
        for row, (raw, gain, out) in enumerate(((kr, gk_ref, kn), (qr, gq_ref, qn))):
            row = 1 - row
            wide = jnp.broadcast_to(factor[row : row + 1], (HEAD_DIM, cap)).T
            for c in range(heads):
                cols = slice(c * HEAD_DIM, (c + 1) * HEAD_DIM)
                out[:, cols] = (raw[:, cols].astype(F32) * wide * gain[cols].reshape(1, HEAD_DIM)).astype(BF16)
        loads[4].wait()
        place = lax.broadcasted_iota(jnp.int32, (EDGE, cap), 0) + (length - EDGE)
        pick = (lax.broadcasted_iota(jnp.int32, (EDGE, cap), 1) == place).astype(F32).astype(BF16)
        tail[0] = jnp.dot(pick, kn[...], preferred_element_type=F32).astype(BF16)
        tail[1] = jnp.dot(pick, vr[...], preferred_element_type=F32).astype(BF16)

        @pl.when(t < tiles - 1)
        def _():
            for x in range(2):
                edge(0, x).start()

        @pl.when(t > 0)
        def _():
            for x in range(2):
                edge(1, x).start()

    def update(i, keys, values, bias):
        cols = pl.ds(pl.multiple_of(i * HEAD_DIM, HEAD_DIM), HEAD_DIM)
        scores = lax.dot_general(qn[:, cols], keys(cols), (((1,), (1,)), ((), ())), preferred_element_type=F32)
        scores = scores * SCORE_SCALE + bias
        before = mx[i]
        now = jnp.maximum(before, jnp.max(scores, axis=1, keepdims=True))
        expo = jnp.exp2(scores - now[:, :1])
        keep = jnp.exp2(before - now)
        mx[i] = now
        ls[i] = ls[i] * keep + jnp.sum(expo, axis=1, keepdims=True)
        acc[i] = acc[i] * keep + jnp.dot(expo.astype(BF16), values(cols), preferred_element_type=F32)

    def own_attention(i):
        spot = lax.broadcasted_iota(jnp.int32, (1, cap), 1)
        ok_own = jnp.where(spot < length, 0.0, NEG).astype(F32)
        slot = lax.broadcasted_iota(jnp.int32, (1, 2 * EDGE), 1)
        ll, lsess = mrecv[0, 0:1, :], mrecv[0, 1:2, :]
        rl, rsess = mrecv[1, 0:1, :], mrecv[1, 1:2, :]
        from_left = (slot < EDGE) & (lsess == jnp.where(t > 0, session, -1)) & (slot >= EDGE - ll)
        from_right = (slot >= EDGE) & (rsess == jnp.where(t < tiles - 1, session, -1)) & (slot - EDGE < rl)
        ok_edge = jnp.where(from_left | from_right, 0.0, NEG).astype(F32)
        update(
            i,
            lambda c: jnp.concatenate([kn[:, c], ekv[0, 0, :, c], ekv[1, 0, :, c]], 0),
            lambda c: jnp.concatenate([vr[:, c], ekv[0, 1, :, c], ekv[1, 1, :, c]], 0),
            jnp.concatenate([ok_own, ok_edge], 1),
        )

    def origin(r):
        return lax.rem(z + nz - r, nz)

    def hand_out(r, x, src, rels=(2, 3, 1, 0)):
        owner = origin(r) * 4 + sub
        for rel in rels:
            out = (mkk, mvv)[x].at[r, pl.ds(0, 2)] if rel == 0 else sel.at[(x * 3 + rel - 1) * nz + r]
            for slot in range(2):
                out[slot] = src[jnp.maximum(snear[rel, slot, owner], 0)]
            if rel > 0:
                pltpu.make_async_remote_copy(
                    src_ref=sel.at[(x * 3 + rel - 1) * nz + r], dst_ref=(mkk, mvv)[x].at[r, pl.ds(2 * rel, 2)],
                    send_sem=out_sem.at[6], recv_sem=near_sem.at[r],
                    device_id={"tile": near(rel)}, device_id_type=MESH).start()

    def far_out(d, x, src, rels):
        owner = origin(full if d == 0 else nz - full) * 4 + sub
        for far_by in (2, 1) if d == x else (1,):
            i, r = (far_by - 1) * 2 + d, (full + far_by) if d == 0 else nz - full - far_by
            for rel in rels:
                place = (d * 2 + x if far_by == 1 else 4 + d) * 4 + rel
                for slot in range(2):
                    far[place, slot] = src[jnp.maximum(sfar[i * 4 + rel, slot, owner], 0)]
                pltpu.make_async_remote_copy(
                    src_ref=far.at[place], dst_ref=(mkk, mvv)[x].at[r, pl.ds(2 * rel, 2)],
                    send_sem=out_sem.at[7], recv_sem=near_sem.at[r],
                    device_id={"tile": at(steps[i], rel)}, device_id_type=MESH).start()

    def chunk(slots, beyond, loop):
        for r in slots:
            away = beyond and isinstance(r, int) and full < r < nz - full
            landed(sel.at[pl.ds(0, 8 if away else 6)], near_sem.at[r])
        group = lane // 8
        biases = []
        for pair_of in (slots[i : i + 2] for i in range(0, len(slots), 2)):
            bias = jnp.full((1, 128), NEG, F32)
            for j, r in enumerate(pair_of):
                for rel in range(4):
                    for slot in range(2):
                        want = snear[0, slot, origin(r) * 4 + near(rel) - z * 4]
                        miss = jnp.where(want < 0, NEG, 0.0).astype(F32)
                        bias = jnp.where(group == j * 8 + rel * 2 + slot, miss, bias)
            biases.append(bias[:, : 64 * len(pair_of)])
        bias = biases[0] if len(biases) == 1 else jnp.concatenate(biases, 1)

        def rows(ref, c):
            return jnp.concatenate([ref[r, :, :, c].reshape(64, HEAD_DIM) for r in slots], 0)

        def one(i):
            update(i, lambda c: rows(mkk, c), lambda c: rows(mvv, c), bias)

        if loop:
            pl.loop(0, heads)(one)
        else:
            for i in range(heads):
                one(i)

    loads[2].wait()
    loads[3].wait()
    cur_ka[...] = kvb[0]
    cur_va[...] = kvb[nz]
    hand_out(0, 0, cur_ka)
    hand_out(0, 1, cur_va)

    def arrived(s, x):
        for d in range(2):
            hop(d, s, x).wait_recv()
            hop(d, s + 1, x).start()

    def take(s, x):
        up_cur, dn_cur = ((cur_ka, cur_kb), (cur_va, cur_vb))[x]
        up_cur[...] = kvb[x * nz + s]
        dn_cur[...] = kvb[x * nz + nz - s]
        hand_out(s, x, up_cur)
        hand_out(nz - s, x, dn_cur)

    def halves():
        landed(sbuf.at[pl.ds(0, nh // 2 - 1)], table_sem.at[3])
        total = sbuf[0]
        for i in range(1, nh // 2):
            total = total + sbuf[i]
        shalf[...] = total
        pair.start()

    arrived(1, 0)
    take(1, 0)
    halves()
    arrived(1, 1)
    take(1, 1)
    normalise()
    arrived(2, 0)
    take(2, 0)
    chunk((0,), False, True)
    arrived(2, 1)
    take(2, 1)
    chunk((1, nz - 1), False, True)
    @pl.loop(3, full)
    def _(s):
        arrived(s, 0)
        take(s, 0)
        arrived(s, 1)
        take(s, 1)
        chunk((s - 1, nz - s + 1), False, True)

    landed(wfar, table_sem.at[1])
    copy = pltpu.make_async_copy(wfar, sfar, tab_loc.at[1])
    copy.start()
    copy.wait()
    for x, (up_cur, dn_cur) in enumerate(((cur_ka, cur_kb), (cur_va, cur_vb))):
        hop(0, full, x).wait_recv()
        hop(1, full, x).wait_recv()
        up_cur[...] = kvb[x * nz + full]
        dn_cur[...] = kvb[x * nz + nz - full]
        far_out(0, x, up_cur, (2, 3))
        far_out(1, x, dn_cur, (2, 3))
        far_out(0, x, up_cur, (0, 1))
        far_out(1, x, dn_cur, (0, 1))
        hand_out(full, x, up_cur)
        hand_out(nz - full, x, dn_cur)
    chunk((full - 1, nz - full + 1), False, True)
    landed(mrecv, table_sem.at[2])
    for side, there in ((0, t > 0), (1, t < tiles - 1)):

        @pl.when(there)
        def _(side=side):
            landed(ekv.at[side], edge_in.at[side])

    for i in range(heads):
        own_attention(i)
    chunk((full, nz - full, half - 1, nz - half + 1, half), True, False)
    for i in range(heads):
        o_ref[:, i * HEAD_DIM : (i + 1) * HEAD_DIM] = (acc[i] / ls[i]).astype(BF16)

    landed(kvb.at[pl.ds(0, 4 * full)], out_sem.at[0])
    landed(wnear.at[pl.ds(0, 3)], out_sem.at[1])
    landed(wfar, out_sem.at[2])
    landed(mrecv, out_sem.at[3])
    landed(sbuf.at[pl.ds(0, nh // 2 - 1)], out_sem.at[4])
    pair.wait_send()
    landed(sel.at[pl.ds(0, 6 * (2 * full + 1))], out_sem.at[6])
    landed(far, out_sem.at[7])
    for side, there in ((0, t < tiles - 1), (1, t > 0)):

        @pl.when(there)
        def _(side=side):
            landed(ekv.at[side], edge_out.at[side])


def per_device(tiles, nh, width, q, k, v, gq, gk, mk, mv, tile_len, session, owner, index):
    nz, half = tiles // 4, tiles // 8
    (cap, wid), (blocks, rows, _) = q.shape, mk.shape
    heads = wid // HEAD_DIM
    smem = pl.BlockSpec(memory_space=pltpu.SMEM)
    vmem = pl.BlockSpec(memory_space=pltpu.VMEM)
    hbm = pl.BlockSpec(memory_space=pltpu.HBM)
    sem = pltpu.SemaphoreType.DMA
    tile = pltpu.VMEM((cap, wid), BF16)
    state = pltpu.VMEM((heads, cap, HEAD_DIM), F32)
    block = pltpu.VMEM((blocks, rows, wid), BF16)
    attended = pl.pallas_call(
        functools.partial(kernel, tiles, nh, width),
        out_shape=jax.ShapeDtypeStruct((cap, wid), BF16),
        in_specs=[smem] * 2 + [hbm] * 9,
        out_specs=vmem,
        scratch_shapes=[
            pltpu.VMEM((2 * nz, blocks, rows, wid), BF16),
            block, block, block, block,
            tile, tile, tile, tile, tile,
            pltpu.VMEM((wid,), F32),
            pltpu.VMEM((wid,), F32),
            pltpu.SMEM(index.shape, jnp.int32),
            pltpu.SMEM(index.shape, jnp.int32),
            pltpu.VMEM((2, cap), F32),
            pltpu.VMEM((nh // 2, 2, cap), F32),
            pltpu.VMEM((2, cap), F32),
            pltpu.VMEM((2, cap), F32),
            pltpu.VMEM((4, 2, 128), jnp.int32),
            pltpu.VMEM((16, 2, 128), jnp.int32),
            pltpu.VMEM((2, 128), jnp.int32),
            pltpu.VMEM((2, 2, 128), jnp.int32),
            pltpu.SMEM((4, 2, 128), jnp.int32),
            pltpu.SMEM((16, 2, 128), jnp.int32),
            pltpu.VMEM((2, EDGE, wid), BF16),
            pltpu.VMEM((2, 2, EDGE, wid), BF16),
            pltpu.VMEM((6 * nz, 2, rows, wid), BF16),
            pltpu.VMEM((24, 2, rows, wid), BF16),
            pltpu.VMEM((nz, 8, rows, wid), BF16),
            pltpu.VMEM((nz, 8, rows, wid), BF16),
            state, state, state,
            sem((8,)), sem((2, half - 2, 2)), sem((9,)), sem((5,)), sem((nz,)), sem((2,)), sem((2,)), sem((2,)),
        ],
        compiler_params=pltpu.CompilerParams(
            collective_id=0, has_side_effects=True, vmem_limit_bytes=44 * 1024 * 1024
        ),
        name="tile_attention",
    )(
        tile_len, session, *(pltpu.with_memory_space_constraint(a, pltpu.HBM) for a in (owner.reshape(-1), index, gq, gk, q, k, v, mk, mv)),
    )
    live = lax.broadcasted_iota(jnp.int32, (cap, wid), 0) < tile_len[0]
    return jnp.where(live, attended, jnp.bfloat16(0))


def solution(mesh):
    in_specs = (
        P("tile", "head"),
        P("tile", "head"),
        P("tile", "head"),
        P("head"),
        P("head"),
        P("tile", None, "head"),
        P("tile", None, "head"),
        P("tile"),
        P("tile"),
        P("tile", None),
        P("tile"),
    )
    tiles, nh = mesh.shape["tile"], mesh.shape["head"]

    def whole(q, *rest):
        body = functools.partial(per_device, tiles, nh, q.shape[1])
        return jax.shard_map(
            body, mesh=mesh, in_specs=in_specs, out_specs=P("tile", "head"), check_vma=False
        )(q, *rest)

    return whole
```

```python
import functools
import math

import jax
import jax.numpy as jnp
from jax import lax
from jax.experimental import pallas as pl
from jax.experimental.pallas import tpu as pltpu
from jax.sharding import PartitionSpec as P

HEAD_DIM = 128
EDGE = 64
EPSILON = 1e-06
MESH = pl.DeviceIdType.MESH
NEG = -1e30
BF16 = jnp.bfloat16
F32 = jnp.float32
SCORE_SCALE = (1.0 / HEAD_DIM**0.5) * math.log2(math.e)
LAST_GROUPS = ((0, 1), (2, 3), (4,))


def kernel(
    tiles, nh, width,
    len_ref, ses_ref, own_hbm, idx_hbm, gq_hbm, gk_hbm,
    q_hbm, k_hbm, v_hbm, mk_hbm, mv_hbm, o_ref,
    kvb, cur_ka, cur_va, cur_kb, cur_vb,
    qr, kr, vr, qn, kn,
    gq_ref, gk_ref, own_ref, idx_ref,
    ssrc, sbuf, shalf, sother, wnear, wfar, msrc, mrecv, snear, sfar,
    tail, ekv, sel, far, mkk, mvv,
    acc, mx, ls,
    out_sem, hop_sem, loc, table_sem, near_sem, edge_out, edge_in, tab_loc,
):
    nz, half = tiles // 4, tiles // 8
    full = half - 2
    cap, wid = qr.shape
    heads = wid // HEAD_DIM
    t, h = lax.axis_index("tile"), lax.axis_index("head")
    z, sub = t // 4, lax.rem(t, 4)
    up, dn = lax.rem(t + 4, tiles), lax.rem(t + tiles - 4, tiles)
    right, left = lax.rem(t + 1, tiles), lax.rem(t + tiles - 1, tiles)

    def near(rel):
        other = sub + jnp.where(lax.rem(sub, 2) == 0, 1, -1) * (rel % 2)
        other = other + jnp.where(sub // 2 == 0, 2, -2) * (rel // 2)
        return z * 4 + other

    def landed(ref, semaphore):
        pltpu.make_async_copy(ref, ref, semaphore).wait()

    bar = pltpu.get_barrier_semaphore()
    steps = (1, -1, 2, -2)

    def at(dz, rel):
        return lax.rem(z + dz + nz, nz) * 4 + near(rel) - z * 4

    greet = [{"tile": up}, {"tile": dn}] + [{"tile": near(rel)} for rel in range(1, 4)]
    greet += [{"head": lax.rem(h + 2 * i, nh)} for i in range(1, nh // 2)]
    hpair = h + jnp.where(lax.rem(h, 2) == 0, 1, -1)
    greet += [{"head": hpair}]
    for n in greet:
        pl.semaphore_signal(bar, inc=1, device_id=n, device_id_type=MESH)
    pl.semaphore_wait(bar, len(greet))

    def hop(d, s, x):
        first = (mk_hbm, mv_hbm)[x]
        static = isinstance(s, int)
        if d == 0:
            src, dst, dev = s - 1, s, up
        else:
            src, dst, dev = nz + 1 - s, nz - s, dn
        return pltpu.make_async_remote_copy(
            src_ref=first if static and s == 1 else kvb.at[x * nz + src], dst_ref=kvb.at[x * nz + dst],
            send_sem=out_sem.at[0], recv_sem=hop_sem.at[d, s - 1, x],
            device_id={"tile": dev}, device_id_type=MESH)

    for x in range(2):
        for d in range(2):
            hop(d, 1, x).start()

    loads = [
        pltpu.make_async_copy(a, b, loc.at[i])
        for i, (a, b) in enumerate((
            (q_hbm, qr), (k_hbm, kr), (mk_hbm, kvb.at[0]), (mv_hbm, kvb.at[nz]), (v_hbm, vr),
            (gq_hbm, gq_ref), (gk_hbm, gk_ref), (own_hbm, own_ref), (idx_hbm, idx_ref),
        ))
    ]
    for i in (7, 8, 0, 1, 2, 3, 4, 5, 6):
        loads[i].start()

    lane = lax.broadcasted_iota(jnp.int32, (1, 128), 1)

    def ask(r, carry):
        w0, w1 = carry
        hit, b = lane == own_ref[r], idx_ref[r]
        return (
            jnp.where(jnp.logical_and(hit, w0 < 0), b, w0),
            jnp.where(jnp.logical_and(hit, w0 >= 0), b, w1),
        )

    none = jnp.full((1, 128), -1, jnp.int32)
    loads[7].wait()
    loads[8].wait()
    w0, w1 = lax.fori_loop(0, own_ref.shape[0], ask, (none, none))
    length, session = len_ref[0], ses_ref[0]
    wnear[0, 0:1, :] = w0
    wnear[0, 1:2, :] = w1
    msrc[0:1, :] = jnp.full((1, 128), length, jnp.int32)
    msrc[1:2, :] = jnp.full((1, 128), session, jnp.int32)

    def tell(rel):
        return pltpu.make_async_remote_copy(
            src_ref=wnear.at[0], dst_ref=wnear.at[rel], send_sem=out_sem.at[1], recv_sem=table_sem.at[0],
            device_id={"tile": near(rel)}, device_id_type=MESH)

    def tell_far(i, far):
        dst = wfar.at[pl.ds((i ^ 1) * 4 + 8 * far, 4)]
        return pltpu.make_async_remote_copy(
            src_ref=wfar.at[pl.ds((i ^ 1) * 4, 4)] if far else wnear, dst_ref=dst,
            send_sem=out_sem.at[2], recv_sem=table_sem.at[5 if far else 1],
            device_id={"tile": (up, dn)[i]}, device_id_type=MESH)

    def meta(side):
        return pltpu.make_async_remote_copy(
            src_ref=msrc, dst_ref=mrecv.at[side], send_sem=out_sem.at[3], recv_sem=table_sem.at[2],
            device_id={"tile": (right, left)[side]}, device_id_type=MESH)

    for rel in range(1, 4):
        tell(rel).start()

    loads[0].wait()
    loads[1].wait()

    def square_row(ref):
        part = jnp.zeros((cap, HEAD_DIM), F32)
        for c in range(heads):
            x = ref[:, c * HEAD_DIM : (c + 1) * HEAD_DIM].astype(F32)
            part = part + x * x
        return jnp.sum(part.T, axis=0, keepdims=True)

    ssrc[0:1, :] = square_row(qr)
    ssrc[1:2, :] = square_row(kr)
    sbuf[h // 2] = ssrc[...]

    def share(i):
        return pltpu.make_async_remote_copy(
            src_ref=ssrc, dst_ref=sbuf.at[h // 2], send_sem=out_sem.at[4], recv_sem=table_sem.at[3],
            device_id={"head": lax.rem(h + 2 * i, nh)}, device_id_type=MESH)

    for i in range(1, nh // 2):
        share(i).start()

    pair = pltpu.make_async_remote_copy(
        src_ref=shalf, dst_ref=sother, send_sem=out_sem.at[5], recv_sem=table_sem.at[4],
        device_id={"head": hpair}, device_id_type=MESH)

    for i in range(heads):
        acc[i] = jnp.zeros((cap, HEAD_DIM), F32)
        mx[i] = jnp.full((cap, HEAD_DIM), NEG, F32)
        ls[i] = jnp.zeros((cap, HEAD_DIM), F32)

    @pl.when(t == 0)
    def _():
        ekv[0] = jnp.zeros((2, EDGE, wid), BF16)

    @pl.when(t == tiles - 1)
    def _():
        ekv[1] = jnp.zeros((2, EDGE, wid), BF16)

    landed(wnear.at[pl.ds(1, 3)], table_sem.at[0])
    copy = pltpu.make_async_copy(wnear, snear, tab_loc.at[0])
    copy.start()
    for i in range(2):
        tell_far(i, False).start()
    copy.wait()

    def edge(side, x):
        src = (tail.at[x], (kn, vr)[x].at[pl.ds(0, EDGE)])[side]
        return pltpu.make_async_remote_copy(
            src_ref=src, dst_ref=ekv.at[side, x], send_sem=edge_out.at[side], recv_sem=edge_in.at[side],
            device_id={"tile": (right, left)[side]}, device_id_type=MESH)

    def normalise():
        pair.wait_recv()
        loads[5].wait()
        loads[6].wait()
        factor = lax.rsqrt((shalf[...] + sother[...]) / width + EPSILON)
        for row, (raw, gain, out) in enumerate(((kr, gk_ref, kn), (qr, gq_ref, qn))):
            row = 1 - row
            wide = jnp.broadcast_to(factor[row : row + 1], (HEAD_DIM, cap)).T
            for c in range(heads):
                cols = slice(c * HEAD_DIM, (c + 1) * HEAD_DIM)
                out[:, cols] = (raw[:, cols].astype(F32) * wide * gain[cols].reshape(1, HEAD_DIM)).astype(BF16)
        loads[4].wait()
        place = lax.broadcasted_iota(jnp.int32, (EDGE, cap), 0) + (length - EDGE)
        pick = (lax.broadcasted_iota(jnp.int32, (EDGE, cap), 1) == place).astype(F32).astype(BF16)
        tail[0] = jnp.dot(pick, kn[...], preferred_element_type=F32).astype(BF16)
        tail[1] = jnp.dot(pick, vr[...], preferred_element_type=F32).astype(BF16)

        @pl.when(t < tiles - 1)
        def _():
            for x in range(2):
                edge(0, x).start()

        @pl.when(t > 0)
        def _():
            for x in range(2):
                edge(1, x).start()

    def update(i, keys, values, bias):
        cols = pl.ds(pl.multiple_of(i * HEAD_DIM, HEAD_DIM), HEAD_DIM)
        scores = lax.dot_general(qn[:, cols], keys(cols), (((1,), (1,)), ((), ())), preferred_element_type=F32)
        scores = scores * SCORE_SCALE + bias
        before = mx[i]
        now = jnp.maximum(before, jnp.max(scores, axis=1, keepdims=True))
        expo = jnp.exp2(scores - now[:, :1])
        keep = jnp.exp2(before - now)
        mx[i] = now
        ls[i] = ls[i] * keep + jnp.sum(expo, axis=1, keepdims=True)
        acc[i] = acc[i] * keep + jnp.dot(expo.astype(BF16), values(cols), preferred_element_type=F32)

    def own_attention(i):
        spot = lax.broadcasted_iota(jnp.int32, (1, cap), 1)
        ok_own = jnp.where(spot < length, 0.0, NEG).astype(F32)
        slot = lax.broadcasted_iota(jnp.int32, (1, 2 * EDGE), 1)
        ll, lsess = mrecv[0, 0:1, :], mrecv[0, 1:2, :]
        rl, rsess = mrecv[1, 0:1, :], mrecv[1, 1:2, :]
        from_left = (slot < EDGE) & (lsess == jnp.where(t > 0, session, -1)) & (slot >= EDGE - ll)
        from_right = (slot >= EDGE) & (rsess == jnp.where(t < tiles - 1, session, -1)) & (slot - EDGE < rl)
        ok_edge = jnp.where(from_left | from_right, 0.0, NEG).astype(F32)
        update(
            i,
            lambda c: jnp.concatenate([kn[:, c], ekv[0, 0, :, c], ekv[1, 0, :, c]], 0),
            lambda c: jnp.concatenate([vr[:, c], ekv[0, 1, :, c], ekv[1, 1, :, c]], 0),
            jnp.concatenate([ok_own, ok_edge], 1),
        )

    def origin(r):
        return lax.rem(z + nz - r, nz)

    def hand_out(r, x, src, rels=(2, 3, 1, 0)):
        owner = origin(r) * 4 + sub
        for rel in rels:
            out = (mkk, mvv)[x].at[r, pl.ds(0, 2)] if rel == 0 else sel.at[(x * 3 + rel - 1) * nz + r]
            for slot in range(2):
                out[slot] = src[jnp.maximum(snear[rel, slot, owner], 0)]
            if rel > 0:
                pltpu.make_async_remote_copy(
                    src_ref=sel.at[(x * 3 + rel - 1) * nz + r], dst_ref=(mkk, mvv)[x].at[r, pl.ds(2 * rel, 2)],
                    send_sem=out_sem.at[6], recv_sem=near_sem.at[r],
                    device_id={"tile": near(rel)}, device_id_type=MESH).start()

    def far_out(d, x, src, rels):
        owner = origin(full if d == 0 else nz - full) * 4 + sub
        for far_by in (2, 1) if d == x else (1,):
            i, r = (far_by - 1) * 2 + d, (full + far_by) if d == 0 else nz - full - far_by
            for rel in rels:
                place = (d * 2 + x if far_by == 1 else 4 + d) * 4 + rel
                for slot in range(2):
                    far[place, slot] = src[jnp.maximum(sfar[i * 4 + rel, slot, owner], 0)]
                pltpu.make_async_remote_copy(
                    src_ref=far.at[place], dst_ref=(mkk, mvv)[x].at[r, pl.ds(2 * rel, 2)],
                    send_sem=out_sem.at[7], recv_sem=near_sem.at[r],
                    device_id={"tile": at(steps[i], rel)}, device_id_type=MESH).start()

    def chunk(slots, beyond, loop):
        for r in slots:
            away = beyond and isinstance(r, int) and full < r < nz - full
            landed(sel.at[pl.ds(0, 8 if away else 6)], near_sem.at[r])
        group = lane // 8
        biases = []
        for pair_of in (slots[i : i + 2] for i in range(0, len(slots), 2)):
            bias = jnp.full((1, 128), NEG, F32)
            for j, r in enumerate(pair_of):
                for rel in range(4):
                    for slot in range(2):
                        want = snear[0, slot, origin(r) * 4 + near(rel) - z * 4]
                        miss = jnp.where(want < 0, NEG, 0.0).astype(F32)
                        bias = jnp.where(group == j * 8 + rel * 2 + slot, miss, bias)
            biases.append(bias[:, : 64 * len(pair_of)])
        bias = biases[0] if len(biases) == 1 else jnp.concatenate(biases, 1)

        def rows(ref, c):
            return jnp.concatenate([ref[r, :, :, c].reshape(64, HEAD_DIM) for r in slots], 0)

        def one(i):
            update(i, lambda c: rows(mkk, c), lambda c: rows(mvv, c), bias)

        if loop:
            pl.loop(0, heads)(one)
            return
        live = lax.broadcasted_iota(jnp.int32, (cap, HEAD_DIM), 0) < length
        for some in LAST_GROUPS:
            cols = [slice(i * HEAD_DIM, (i + 1) * HEAD_DIM) for i in some]
            scores = [
                lax.dot_general(qn[:, c], rows(mkk, c), (((1,), (1,)), ((), ())), preferred_element_type=F32)
                * SCORE_SCALE + bias for c in cols
            ]
            now = [jnp.maximum(mx[i], jnp.max(x, axis=1, keepdims=True)) for i, x in zip(some, scores)]
            expo = [jnp.exp2(x - n[:, :1]) for x, n in zip(scores, now)]
            keep = [jnp.exp2(mx[i] - n) for i, n in zip(some, now)]
            whole = [ls[i] * k + jnp.sum(e, axis=1, keepdims=True) for i, k, e in zip(some, keep, expo)]
            for i, c, k, e, w in zip(some, cols, keep, expo, whole):
                out = acc[i] * k + jnp.dot(e.astype(BF16), rows(mvv, c), preferred_element_type=F32)
                o_ref[:, c] = jnp.where(live, out / w, 0.0).astype(BF16)

    loads[2].wait()
    loads[3].wait()
    cur_ka[...] = kvb[0]
    cur_va[...] = kvb[nz]
    hand_out(0, 0, cur_ka)
    hand_out(0, 1, cur_va)

    def arrived(s, x):
        for d in range(2):
            hop(d, s, x).wait_recv()
            hop(d, s + 1, x).start()

    def take(s, x):
        up_cur, dn_cur = ((cur_ka, cur_kb), (cur_va, cur_vb))[x]
        up_cur[...] = kvb[x * nz + s]
        dn_cur[...] = kvb[x * nz + nz - s]
        hand_out(s, x, up_cur)
        hand_out(nz - s, x, dn_cur)

    def halves():
        landed(sbuf.at[pl.ds(0, nh // 2 - 1)], table_sem.at[3])
        total = sbuf[0]
        for i in range(1, nh // 2):
            total = total + sbuf[i]
        shalf[...] = total
        pair.start()

    arrived(1, 0)
    take(1, 0)
    halves()
    arrived(1, 1)
    landed(wfar.at[pl.ds(0, 8)], table_sem.at[1])
    for i in range(2):
        tell_far(i, True).start()
    meta(0).start()
    meta(1).start()
    take(1, 1)
    normalise()
    arrived(2, 0)
    take(2, 0)
    chunk((0,), False, True)
    arrived(2, 1)
    take(2, 1)
    chunk((1, nz - 1), False, True)
    @pl.loop(3, full)
    def _(s):
        arrived(s, 0)
        take(s, 0)
        arrived(s, 1)
        take(s, 1)
        chunk((s - 1, nz - s + 1), False, True)

    landed(wfar.at[pl.ds(8, 8)], table_sem.at[5])
    copy = pltpu.make_async_copy(wfar, sfar, tab_loc.at[1])
    copy.start()
    copy.wait()
    for x, (up_cur, dn_cur) in enumerate(((cur_ka, cur_kb), (cur_va, cur_vb))):
        hop(0, full, x).wait_recv()
        hop(1, full, x).wait_recv()
        up_cur[...] = kvb[x * nz + full]
        dn_cur[...] = kvb[x * nz + nz - full]
        far_out(0, x, up_cur, (2, 3))
        far_out(1, x, dn_cur, (2, 3))
        far_out(0, x, up_cur, (0, 1))
        far_out(1, x, dn_cur, (0, 1))
        hand_out(full, x, up_cur)
        hand_out(nz - full, x, dn_cur)
    chunk((full - 1, nz - full + 1), False, True)
    landed(mrecv, table_sem.at[2])
    for side, there in ((0, t > 0), (1, t < tiles - 1)):

        @pl.when(there)
        def _(side=side):
            landed(ekv.at[side], edge_in.at[side])

    for i in range(heads):
        own_attention(i)
    chunk((full, nz - full, half - 1, nz - half + 1, half), True, False)
    landed(kvb.at[pl.ds(0, 4 * full)], out_sem.at[0])
    landed(wnear.at[pl.ds(0, 3)], out_sem.at[1])
    landed(wfar, out_sem.at[2])
    landed(mrecv, out_sem.at[3])
    landed(sbuf.at[pl.ds(0, nh // 2 - 1)], out_sem.at[4])
    pair.wait_send()
    landed(sel.at[pl.ds(0, 6 * (2 * full + 1))], out_sem.at[6])
    landed(far, out_sem.at[7])
    for side, there in ((0, t < tiles - 1), (1, t > 0)):

        @pl.when(there)
        def _(side=side):
            landed(ekv.at[side], edge_out.at[side])


def per_device(tiles, nh, width, q, k, v, gq, gk, mk, mv, tile_len, session, owner, index):
    nz, half = tiles // 4, tiles // 8
    (cap, wid), (blocks, rows, _) = q.shape, mk.shape
    heads = wid // HEAD_DIM
    smem = pl.BlockSpec(memory_space=pltpu.SMEM)
    vmem = pl.BlockSpec(memory_space=pltpu.VMEM)
    hbm = pl.BlockSpec(memory_space=pltpu.HBM)
    sem = pltpu.SemaphoreType.DMA
    tile = pltpu.VMEM((cap, wid), BF16)
    state = pltpu.VMEM((heads, cap, HEAD_DIM), F32)
    block = pltpu.VMEM((blocks, rows, wid), BF16)
    return pl.pallas_call(
        functools.partial(kernel, tiles, nh, width),
        out_shape=jax.ShapeDtypeStruct((cap, wid), BF16),
        in_specs=[smem] * 2 + [hbm] * 9,
        out_specs=vmem,
        scratch_shapes=[
            pltpu.VMEM((2 * nz, blocks, rows, wid), BF16),
            block, block, block, block,
            tile, tile, tile, tile, tile,
            pltpu.VMEM((wid,), F32),
            pltpu.VMEM((wid,), F32),
            pltpu.SMEM(index.shape, jnp.int32),
            pltpu.SMEM(index.shape, jnp.int32),
            pltpu.VMEM((2, cap), F32),
            pltpu.VMEM((nh // 2, 2, cap), F32),
            pltpu.VMEM((2, cap), F32),
            pltpu.VMEM((2, cap), F32),
            pltpu.VMEM((4, 2, 128), jnp.int32),
            pltpu.VMEM((16, 2, 128), jnp.int32),
            pltpu.VMEM((2, 128), jnp.int32),
            pltpu.VMEM((2, 2, 128), jnp.int32),
            pltpu.SMEM((4, 2, 128), jnp.int32),
            pltpu.SMEM((16, 2, 128), jnp.int32),
            pltpu.VMEM((2, EDGE, wid), BF16),
            pltpu.VMEM((2, 2, EDGE, wid), BF16),
            pltpu.VMEM((6 * nz, 2, rows, wid), BF16),
            pltpu.VMEM((24, 2, rows, wid), BF16),
            pltpu.VMEM((nz, 8, rows, wid), BF16),
            pltpu.VMEM((nz, 8, rows, wid), BF16),
            state, state, state,
            sem((8,)), sem((2, half - 2, 2)), sem((9,)), sem((6,)), sem((nz,)), sem((2,)), sem((2,)), sem((2,)),
        ],
        compiler_params=pltpu.CompilerParams(
            collective_id=0, has_side_effects=True, vmem_limit_bytes=44 * 1024 * 1024
        ),
        name="tile_attention",
    )(
        tile_len, session, *(pltpu.with_memory_space_constraint(a, pltpu.HBM) for a in (owner.reshape(-1), index, gq, gk, q, k, v, mk, mv)),
    )


def solution(mesh):
    in_specs = (
        P("tile", "head"),
        P("tile", "head"),
        P("tile", "head"),
        P("head"),
        P("head"),
        P("tile", None, "head"),
        P("tile", None, "head"),
        P("tile"),
        P("tile"),
        P("tile", None),
        P("tile"),
    )
    tiles, nh = mesh.shape["tile"], mesh.shape["head"]

    def whole(q, *rest):
        body = functools.partial(per_device, tiles, nh, q.shape[1])
        return jax.shard_map(
            body, mesh=mesh, in_specs=in_specs, out_specs=P("tile", "head"), check_vma=False
        )(q, *rest)

    return whole
```

```python
import functools
import math

import jax
import jax.numpy as jnp
from jax import lax
from jax.experimental import pallas as pl
from jax.experimental.pallas import tpu as pltpu
from jax.sharding import PartitionSpec as P

HEAD_DIM = 128
EDGE = 64
EPSILON = 1e-06
MESH = pl.DeviceIdType.MESH
NEG = -1e30
BF16 = jnp.bfloat16
F32 = jnp.float32
SCORE_SCALE = (1.0 / HEAD_DIM**0.5) * math.log2(math.e)
LAST_GROUPS = ((0, 1), (2, 3), (4,))


def kernel(
    tiles, nh, width,
    len_ref, ses_ref, own_hbm, idx_hbm, gq_hbm, gk_hbm,
    q_hbm, k_hbm, v_hbm, mk_hbm, mv_hbm, o_ref,
    kvb, cur_ka, cur_va, cur_kb, cur_vb,
    qr, kr, vr, qn, kn,
    gq_ref, gk_ref, own_ref, idx_ref,
    ssrc, sbuf, shalf, sother, wnear, wfar, msrc, mrecv, snear, sfar,
    tail, ekv, sel, far, mkk, mvv,
    acc, mx, ls,
    out_sem, hop_sem, loc, table_sem, near_sem, edge_out, edge_in, tab_loc,
):
    nz, half = tiles // 4, tiles // 8
    full = half - 2
    cap, wid = qr.shape
    heads = wid // HEAD_DIM
    t, h = lax.axis_index("tile"), lax.axis_index("head")
    z, sub = t // 4, lax.rem(t, 4)
    up, dn = lax.rem(t + 4, tiles), lax.rem(t + tiles - 4, tiles)
    right, left = lax.rem(t + 1, tiles), lax.rem(t + tiles - 1, tiles)

    def near(rel):
        other = sub + jnp.where(lax.rem(sub, 2) == 0, 1, -1) * (rel % 2)
        other = other + jnp.where(sub // 2 == 0, 2, -2) * (rel // 2)
        return z * 4 + other

    def landed(ref, semaphore):
        pltpu.make_async_copy(ref, ref, semaphore).wait()

    bar = pltpu.get_barrier_semaphore()
    steps = (1, -1, 2, -2)

    def at(dz, rel):
        return lax.rem(z + dz + nz, nz) * 4 + near(rel) - z * 4

    greet = [{"tile": up}, {"tile": dn}] + [{"tile": near(rel)} for rel in range(1, 4)]
    greet += [{"head": lax.rem(h + 2 * i, nh)} for i in range(1, nh // 2)]
    hpair = h + jnp.where(lax.rem(h, 2) == 0, 1, -1)
    greet += [{"head": hpair}]
    for n in greet:
        pl.semaphore_signal(bar, inc=1, device_id=n, device_id_type=MESH)
    loads = [
        pltpu.make_async_copy(a, b, loc.at[i])
        for i, (a, b) in enumerate((
            (q_hbm, qr), (k_hbm, kr), (mk_hbm, kvb.at[0]), (mv_hbm, kvb.at[nz]), (v_hbm, vr),
            (gq_hbm, gq_ref), (gk_hbm, gk_ref), (own_hbm, own_ref), (idx_hbm, idx_ref),
        ))
    ]
    for i in (2, 3, 7, 8, 0, 1, 4, 5, 6):
        loads[i].start()
    pl.semaphore_wait(bar, len(greet))

    def hop(d, s, x):
        if d == 0:
            src, dst, dev = s - 1, s, up
        else:
            src, dst, dev = 0 if isinstance(s, int) and s == 1 else nz + 1 - s, nz - s, dn
        return pltpu.make_async_remote_copy(
            src_ref=kvb.at[x * nz + src], dst_ref=kvb.at[x * nz + dst],
            send_sem=out_sem.at[0], recv_sem=hop_sem.at[d, s - 1, x],
            device_id={"tile": dev}, device_id_type=MESH)

    for x in range(2):
        loads[2 + x].wait()
        for d in range(2):
            hop(d, 1, x).start()

    lane = lax.broadcasted_iota(jnp.int32, (1, 128), 1)

    def ask(r, carry):
        w0, w1 = carry
        hit, b = lane == own_ref[r], idx_ref[r]
        return (
            jnp.where(jnp.logical_and(hit, w0 < 0), b, w0),
            jnp.where(jnp.logical_and(hit, w0 >= 0), b, w1),
        )

    none = jnp.full((1, 128), -1, jnp.int32)
    loads[7].wait()
    loads[8].wait()
    w0, w1 = lax.fori_loop(0, own_ref.shape[0], ask, (none, none))
    length, session = len_ref[0], ses_ref[0]
    wnear[0, 0:1, :] = w0
    wnear[0, 1:2, :] = w1
    msrc[0:1, :] = jnp.full((1, 128), length, jnp.int32)
    msrc[1:2, :] = jnp.full((1, 128), session, jnp.int32)

    def tell(rel):
        return pltpu.make_async_remote_copy(
            src_ref=wnear.at[0], dst_ref=wnear.at[rel], send_sem=out_sem.at[1], recv_sem=table_sem.at[0],
            device_id={"tile": near(rel)}, device_id_type=MESH)

    def tell_far(i, far):
        dst = wfar.at[pl.ds((i ^ 1) * 4 + 8 * far, 4)]
        return pltpu.make_async_remote_copy(
            src_ref=wfar.at[pl.ds((i ^ 1) * 4, 4)] if far else wnear, dst_ref=dst,
            send_sem=out_sem.at[2], recv_sem=table_sem.at[5 if far else 1],
            device_id={"tile": (up, dn)[i]}, device_id_type=MESH)

    def meta(side):
        return pltpu.make_async_remote_copy(
            src_ref=msrc, dst_ref=mrecv.at[side], send_sem=out_sem.at[3], recv_sem=table_sem.at[2],
            device_id={"tile": (right, left)[side]}, device_id_type=MESH)

    for rel in range(1, 4):
        tell(rel).start()

    loads[0].wait()
    loads[1].wait()

    def square_row(ref):
        part = jnp.zeros((cap, HEAD_DIM), F32)
        for c in range(heads):
            x = ref[:, c * HEAD_DIM : (c + 1) * HEAD_DIM].astype(F32)
            part = part + x * x
        return jnp.sum(part.T, axis=0, keepdims=True)

    ssrc[0:1, :] = square_row(qr)
    ssrc[1:2, :] = square_row(kr)
    sbuf[h // 2] = ssrc[...]

    def share(i):
        return pltpu.make_async_remote_copy(
            src_ref=ssrc, dst_ref=sbuf.at[h // 2], send_sem=out_sem.at[4], recv_sem=table_sem.at[3],
            device_id={"head": lax.rem(h + 2 * i, nh)}, device_id_type=MESH)

    for i in range(1, nh // 2):
        share(i).start()

    pair = pltpu.make_async_remote_copy(
        src_ref=shalf, dst_ref=sother, send_sem=out_sem.at[5], recv_sem=table_sem.at[4],
        device_id={"head": hpair}, device_id_type=MESH)

    for i in range(heads):
        acc[i] = jnp.zeros((cap, HEAD_DIM), F32)
        mx[i] = jnp.full((cap, HEAD_DIM), NEG, F32)
        ls[i] = jnp.zeros((cap, HEAD_DIM), F32)

    @pl.when(t == 0)
    def _():
        ekv[0] = jnp.zeros((2, EDGE, wid), BF16)

    @pl.when(t == tiles - 1)
    def _():
        ekv[1] = jnp.zeros((2, EDGE, wid), BF16)

    landed(wnear.at[pl.ds(1, 3)], table_sem.at[0])
    copy = pltpu.make_async_copy(wnear, snear, tab_loc.at[0])
    copy.start()
    for i in range(2):
        tell_far(i, False).start()
    copy.wait()

    def edge(side, x):
        src = (tail.at[x], (kn, vr)[x].at[pl.ds(0, EDGE)])[side]
        return pltpu.make_async_remote_copy(
            src_ref=src, dst_ref=ekv.at[side, x], send_sem=edge_out.at[side], recv_sem=edge_in.at[side],
            device_id={"tile": (right, left)[side]}, device_id_type=MESH)

    def normalise():
        pair.wait_recv()
        loads[5].wait()
        loads[6].wait()
        factor = lax.rsqrt((shalf[...] + sother[...]) / width + EPSILON)
        for row, (raw, gain, out) in enumerate(((kr, gk_ref, kn), (qr, gq_ref, qn))):
            row = 1 - row
            wide = jnp.broadcast_to(factor[row : row + 1], (HEAD_DIM, cap)).T
            for c in range(heads):
                cols = slice(c * HEAD_DIM, (c + 1) * HEAD_DIM)
                out[:, cols] = (raw[:, cols].astype(F32) * wide * gain[cols].reshape(1, HEAD_DIM)).astype(BF16)
        loads[4].wait()
        place = lax.broadcasted_iota(jnp.int32, (EDGE, cap), 0) + (length - EDGE)
        pick = (lax.broadcasted_iota(jnp.int32, (EDGE, cap), 1) == place).astype(F32).astype(BF16)
        tail[0] = jnp.dot(pick, kn[...], preferred_element_type=F32).astype(BF16)
        tail[1] = jnp.dot(pick, vr[...], preferred_element_type=F32).astype(BF16)

        @pl.when(t < tiles - 1)
        def _():
            for x in range(2):
                edge(0, x).start()

        @pl.when(t > 0)
        def _():
            for x in range(2):
                edge(1, x).start()

    def spread(x, width):
        parts = [x] * (width // HEAD_DIM) + ([x[:, : width % HEAD_DIM]] if width % HEAD_DIM else [])
        return parts[0] if len(parts) == 1 else jnp.concatenate(parts, 1)

    def update(i, keys, values, bias):
        cols = pl.ds(pl.multiple_of(i * HEAD_DIM, HEAD_DIM), HEAD_DIM)
        scores = lax.dot_general(qn[:, cols], keys(cols), (((1,), (1,)), ((), ())), preferred_element_type=F32)
        scores = scores * SCORE_SCALE + bias
        before = mx[i]
        now = jnp.maximum(before, jnp.max(scores, axis=1, keepdims=True))
        expo = jnp.exp2(scores - spread(now, scores.shape[1]))
        keep = jnp.exp2(before - now)
        mx[i] = now
        ls[i] = ls[i] * keep + jnp.sum(expo, axis=1, keepdims=True)
        acc[i] = acc[i] * keep + jnp.dot(expo.astype(BF16), values(cols), preferred_element_type=F32)

    def own_attention(i):
        spot = lax.broadcasted_iota(jnp.int32, (1, cap), 1)
        ok_own = jnp.where(spot < length, 0.0, NEG).astype(F32)
        slot = lax.broadcasted_iota(jnp.int32, (1, 2 * EDGE), 1)
        ll, lsess = mrecv[0, 0:1, :], mrecv[0, 1:2, :]
        rl, rsess = mrecv[1, 0:1, :], mrecv[1, 1:2, :]
        from_left = (slot < EDGE) & (lsess == jnp.where(t > 0, session, -1)) & (slot >= EDGE - ll)
        from_right = (slot >= EDGE) & (rsess == jnp.where(t < tiles - 1, session, -1)) & (slot - EDGE < rl)
        ok_edge = jnp.where(from_left | from_right, 0.0, NEG).astype(F32)
        update(
            i,
            lambda c: jnp.concatenate([kn[:, c], ekv[0, 0, :, c], ekv[1, 0, :, c]], 0),
            lambda c: jnp.concatenate([vr[:, c], ekv[0, 1, :, c], ekv[1, 1, :, c]], 0),
            jnp.concatenate([ok_own, ok_edge], 1),
        )

    def origin(r):
        return lax.rem(z + nz - r, nz)

    def hand_out(r, x, src, rels=(2, 3, 1, 0)):
        owner = origin(r) * 4 + sub
        for rel in rels:
            out = (mkk, mvv)[x].at[r, pl.ds(0, 2)] if rel == 0 else sel.at[(x * 3 + rel - 1) * nz + r]
            for slot in range(2):
                out[slot] = src[jnp.maximum(snear[rel, slot, owner], 0)]
            if rel > 0:
                pltpu.make_async_remote_copy(
                    src_ref=sel.at[(x * 3 + rel - 1) * nz + r], dst_ref=(mkk, mvv)[x].at[r, pl.ds(2 * rel, 2)],
                    send_sem=out_sem.at[6], recv_sem=near_sem.at[r],
                    device_id={"tile": near(rel)}, device_id_type=MESH).start()

    def far_out(d, x, src, rels):
        owner = origin(full if d == 0 else nz - full) * 4 + sub
        for far_by in (2, 1) if d == x else (1,):
            i, r = (far_by - 1) * 2 + d, (full + far_by) if d == 0 else nz - full - far_by
            for rel in rels:
                place = (d * 2 + x if far_by == 1 else 4 + d) * 4 + rel
                for slot in range(2):
                    far[place, slot] = src[jnp.maximum(sfar[i * 4 + rel, slot, owner], 0)]
                pltpu.make_async_remote_copy(
                    src_ref=far.at[place], dst_ref=(mkk, mvv)[x].at[r, pl.ds(2 * rel, 2)],
                    send_sem=out_sem.at[7], recv_sem=near_sem.at[r],
                    device_id={"tile": at(steps[i], rel)}, device_id_type=MESH).start()

    def chunk(slots, beyond, loop):
        for r in slots:
            away = beyond and isinstance(r, int) and full < r < nz - full
            landed(sel.at[pl.ds(0, 8 if away else 6)], near_sem.at[r])
        group = lane // 8
        biases = []
        for pair_of in (slots[i : i + 2] for i in range(0, len(slots), 2)):
            bias = jnp.full((1, 128), NEG, F32)
            for j, r in enumerate(pair_of):
                for rel in range(4):
                    for slot in range(2):
                        want = snear[0, slot, origin(r) * 4 + near(rel) - z * 4]
                        miss = jnp.where(want < 0, NEG, 0.0).astype(F32)
                        bias = jnp.where(group == j * 8 + rel * 2 + slot, miss, bias)
            biases.append(bias[:, : 64 * len(pair_of)])
        bias = biases[0] if len(biases) == 1 else jnp.concatenate(biases, 1)

        def rows(ref, c):
            return jnp.concatenate([ref[r, :, :, c].reshape(64, HEAD_DIM) for r in slots], 0)

        def one(i):
            update(i, lambda c: rows(mkk, c), lambda c: rows(mvv, c), bias)

        if loop:
            pl.loop(0, heads)(one)
            return
        live = lax.broadcasted_iota(jnp.int32, (cap, HEAD_DIM), 0) < length
        for some in LAST_GROUPS:
            cols = [slice(i * HEAD_DIM, (i + 1) * HEAD_DIM) for i in some]
            scores = [
                lax.dot_general(qn[:, c], rows(mkk, c), (((1,), (1,)), ((), ())), preferred_element_type=F32)
                * SCORE_SCALE + bias for c in cols
            ]
            now = [jnp.maximum(mx[i], jnp.max(x, axis=1, keepdims=True)) for i, x in zip(some, scores)]
            expo = [jnp.exp2(x - spread(n, x.shape[1])) for x, n in zip(scores, now)]
            keep = [jnp.exp2(mx[i] - n) for i, n in zip(some, now)]
            whole = [ls[i] * k + jnp.sum(e, axis=1, keepdims=True) for i, k, e in zip(some, keep, expo)]
            for i, c, k, e, w in zip(some, cols, keep, expo, whole):
                out = acc[i] * k + jnp.dot(e.astype(BF16), rows(mvv, c), preferred_element_type=F32)
                o_ref[:, c] = jnp.where(live, out / w, 0.0).astype(BF16)

    cur_ka[...] = kvb[0]
    cur_va[...] = kvb[nz]
    hand_out(0, 0, cur_ka)
    hand_out(0, 1, cur_va)

    def arrived(s, x):
        for d in range(2):
            hop(d, s, x).wait_recv()
            hop(d, s + 1, x).start()

    def take(s, x):
        up_cur, dn_cur = ((cur_ka, cur_kb), (cur_va, cur_vb))[x]
        up_cur[...] = kvb[x * nz + s]
        dn_cur[...] = kvb[x * nz + nz - s]
        hand_out(s, x, up_cur)
        hand_out(nz - s, x, dn_cur)

    def halves():
        landed(sbuf.at[pl.ds(0, nh // 2 - 1)], table_sem.at[3])
        total = sbuf[0]
        for i in range(1, nh // 2):
            total = total + sbuf[i]
        shalf[...] = total
        pair.start()

    arrived(1, 0)
    take(1, 0)
    halves()
    arrived(1, 1)
    landed(wfar.at[pl.ds(0, 8)], table_sem.at[1])
    for i in range(2):
        tell_far(i, True).start()
    meta(0).start()
    meta(1).start()
    take(1, 1)
    arrived(2, 0)
    take(2, 0)
    normalise()
    arrived(2, 1)
    take(2, 1)
    chunk((1, nz - 1), False, True)
    @pl.loop(3, full)
    def _(s):
        arrived(s, 0)
        take(s, 0)
        pl.when(s == 3)(lambda: chunk((0,), False, True))
        arrived(s, 1)
        take(s, 1)
        chunk((s - 1, nz - s + 1), False, True)

    landed(wfar.at[pl.ds(8, 8)], table_sem.at[5])
    copy = pltpu.make_async_copy(wfar, sfar, tab_loc.at[1])
    copy.start()
    copy.wait()
    for x, (up_cur, dn_cur) in enumerate(((cur_ka, cur_kb), (cur_va, cur_vb))):
        hop(0, full, x).wait_recv()
        hop(1, full, x).wait_recv()
        up_cur[...] = kvb[x * nz + full]
        dn_cur[...] = kvb[x * nz + nz - full]
        far_out(0, x, up_cur, (2, 3))
        far_out(1, x, dn_cur, (2, 3))
        far_out(0, x, up_cur, (0, 1))
        far_out(1, x, dn_cur, (0, 1))
        hand_out(full, x, up_cur)
        hand_out(nz - full, x, dn_cur)
    chunk((full - 1, nz - full + 1), False, True)
    landed(mrecv, table_sem.at[2])
    for side, there in ((0, t > 0), (1, t < tiles - 1)):

        @pl.when(there)
        def _(side=side):
            landed(ekv.at[side], edge_in.at[side])

    for i in range(heads):
        own_attention(i)
    chunk((full, nz - full, half - 1, nz - half + 1, half), True, False)
    landed(kvb.at[pl.ds(0, 4 * full)], out_sem.at[0])
    landed(wnear.at[pl.ds(0, 3)], out_sem.at[1])
    landed(wfar, out_sem.at[2])
    landed(mrecv, out_sem.at[3])
    landed(sbuf.at[pl.ds(0, nh // 2 - 1)], out_sem.at[4])
    pair.wait_send()
    landed(sel.at[pl.ds(0, 6 * (2 * full + 1))], out_sem.at[6])
    landed(far, out_sem.at[7])
    for side, there in ((0, t < tiles - 1), (1, t > 0)):

        @pl.when(there)
        def _(side=side):
            landed(ekv.at[side], edge_out.at[side])


def per_device(tiles, nh, width, q, k, v, gq, gk, mk, mv, tile_len, session, owner, index):
    nz, half = tiles // 4, tiles // 8
    (cap, wid), (blocks, rows, _) = q.shape, mk.shape
    heads = wid // HEAD_DIM
    smem = pl.BlockSpec(memory_space=pltpu.SMEM)
    vmem = pl.BlockSpec(memory_space=pltpu.VMEM)
    hbm = pl.BlockSpec(memory_space=pltpu.HBM)
    sem = pltpu.SemaphoreType.DMA
    tile = pltpu.VMEM((cap, wid), BF16)
    state = pltpu.VMEM((heads, cap, HEAD_DIM), F32)
    block = pltpu.VMEM((blocks, rows, wid), BF16)
    return pl.pallas_call(
        functools.partial(kernel, tiles, nh, width),
        out_shape=jax.ShapeDtypeStruct((cap, wid), BF16),
        in_specs=[smem] * 2 + [hbm] * 9,
        out_specs=vmem,
        scratch_shapes=[
            pltpu.VMEM((2 * nz, blocks, rows, wid), BF16),
            block, block, block, block,
            tile, tile, tile, tile, tile,
            pltpu.VMEM((wid,), F32),
            pltpu.VMEM((wid,), F32),
            pltpu.SMEM(index.shape, jnp.int32),
            pltpu.SMEM(index.shape, jnp.int32),
            pltpu.VMEM((2, cap), F32),
            pltpu.VMEM((nh // 2, 2, cap), F32),
            pltpu.VMEM((2, cap), F32),
            pltpu.VMEM((2, cap), F32),
            pltpu.VMEM((4, 2, 128), jnp.int32),
            pltpu.VMEM((16, 2, 128), jnp.int32),
            pltpu.VMEM((2, 128), jnp.int32),
            pltpu.VMEM((2, 2, 128), jnp.int32),
            pltpu.SMEM((4, 2, 128), jnp.int32),
            pltpu.SMEM((16, 2, 128), jnp.int32),
            pltpu.VMEM((2, EDGE, wid), BF16),
            pltpu.VMEM((2, 2, EDGE, wid), BF16),
            pltpu.VMEM((6 * nz, 2, rows, wid), BF16),
            pltpu.VMEM((24, 2, rows, wid), BF16),
            pltpu.VMEM((nz, 8, rows, wid), BF16),
            pltpu.VMEM((nz, 8, rows, wid), BF16),
            state, state, state,
            sem((8,)), sem((2, half - 2, 2)), sem((9,)), sem((6,)), sem((nz,)), sem((2,)), sem((2,)), sem((2,)),
        ],
        compiler_params=pltpu.CompilerParams(
            collective_id=0, has_side_effects=True, vmem_limit_bytes=44 * 1024 * 1024
        ),
        name="tile_attention",
    )(
        tile_len, session, *(pltpu.with_memory_space_constraint(a, pltpu.HBM) for a in (owner.reshape(-1), index, gq, gk, q, k, v, mk, mv)),
    )


def solution(mesh):
    in_specs = (
        P("tile", "head"),
        P("tile", "head"),
        P("tile", "head"),
        P("head"),
        P("head"),
        P("tile", None, "head"),
        P("tile", None, "head"),
        P("tile"),
        P("tile"),
        P("tile", None),
        P("tile"),
    )
    tiles, nh = mesh.shape["tile"], mesh.shape["head"]

    def whole(q, *rest):
        body = functools.partial(per_device, tiles, nh, q.shape[1])
        return jax.shard_map(
            body, mesh=mesh, in_specs=in_specs, out_specs=P("tile", "head"), check_vma=False
        )(q, *rest)

    return whole
```

```python
import functools
import math

import jax
import jax.numpy as jnp
from jax import lax
from jax.experimental import pallas as pl
from jax.experimental.pallas import tpu as pltpu
from jax.sharding import PartitionSpec as P

HEAD_DIM = 128
EDGE = 64
EPSILON = 1e-06
MESH = pl.DeviceIdType.MESH
NEG = -1e30
BF16 = jnp.bfloat16
F32 = jnp.float32
SCORE_SCALE = (1.0 / HEAD_DIM**0.5) * math.log2(math.e)
LAST_GROUPS = ((0, 1, 2), (3, 4))


def kernel(
    tiles, nh, width,
    len_ref, ses_ref, own_hbm, idx_hbm, gq_hbm, gk_hbm,
    q_hbm, k_hbm, v_hbm, mk_hbm, mv_hbm, o_ref,
    kvb, cur_ka, cur_va, cur_kb, cur_vb,
    qr, kr, vr, qn, kn,
    gq_ref, gk_ref, own_ref, idx_ref,
    ssrc, sbuf, shalf, sother, wnear, wfar, msrc, mrecv, snear, sfar,
    tail, ekv, sel, far, mkk, mvv,
    acc, mx, ls,
    out_sem, hop_sem, loc, table_sem, near_sem, edge_out, edge_in, tab_loc,
):
    nz, half = tiles // 4, tiles // 8
    full = half - 2
    cap, wid = qr.shape
    heads = wid // HEAD_DIM
    t, h = lax.axis_index("tile"), lax.axis_index("head")
    z, sub = t // 4, lax.rem(t, 4)
    up, dn = lax.rem(t + 4, tiles), lax.rem(t + tiles - 4, tiles)
    right, left = lax.rem(t + 1, tiles), lax.rem(t + tiles - 1, tiles)

    def near(rel):
        other = sub + jnp.where(lax.rem(sub, 2) == 0, 1, -1) * (rel % 2)
        other = other + jnp.where(sub // 2 == 0, 2, -2) * (rel // 2)
        return z * 4 + other

    def landed(ref, semaphore):
        pltpu.make_async_copy(ref, ref, semaphore).wait()

    bar = pltpu.get_barrier_semaphore()
    steps = (1, -1, 2, -2)

    def at(dz, rel):
        return lax.rem(z + dz + nz, nz) * 4 + near(rel) - z * 4

    greet = [{"tile": up}, {"tile": dn}] + [{"tile": near(rel)} for rel in range(1, 4)]
    greet += [{"head": lax.rem(h + 2 * i, nh)} for i in range(1, nh // 2)]
    hpair = h + jnp.where(lax.rem(h, 2) == 0, 1, -1)
    greet += [{"head": hpair}]
    for n in greet:
        pl.semaphore_signal(bar, inc=1, device_id=n, device_id_type=MESH)
    loads = [
        pltpu.make_async_copy(a, b, loc.at[i])
        for i, (a, b) in enumerate((
            (q_hbm, qr), (k_hbm, kr), (mk_hbm, kvb.at[0]), (mv_hbm, kvb.at[nz]), (v_hbm, vr),
            (gq_hbm, gq_ref), (gk_hbm, gk_ref), (own_hbm, own_ref), (idx_hbm, idx_ref),
        ))
    ]
    for i in (2, 3, 7, 8, 0, 1, 4, 5, 6):
        loads[i].start()
    pl.semaphore_wait(bar, len(greet))

    def hop(d, s, x):
        if d == 0:
            src, dst, dev = s - 1, s, up
        else:
            src, dst, dev = 0 if isinstance(s, int) and s == 1 else nz + 1 - s, nz - s, dn
        return pltpu.make_async_remote_copy(
            src_ref=kvb.at[x * nz + src], dst_ref=kvb.at[x * nz + dst],
            send_sem=out_sem.at[0], recv_sem=hop_sem.at[d, s - 1, x],
            device_id={"tile": dev}, device_id_type=MESH)

    for x in range(2):
        loads[2 + x].wait()
        for d in range(2):
            hop(d, 1, x).start()

    lane = lax.broadcasted_iota(jnp.int32, (1, 128), 1)

    def ask(r, carry):
        w0, w1 = carry
        hit, b = lane == own_ref[r], idx_ref[r]
        return (
            jnp.where(jnp.logical_and(hit, w0 < 0), b, w0),
            jnp.where(jnp.logical_and(hit, w0 >= 0), b, w1),
        )

    none = jnp.full((1, 128), -1, jnp.int32)
    loads[7].wait()
    loads[8].wait()
    w0, w1 = lax.fori_loop(0, own_ref.shape[0], ask, (none, none))
    length, session = len_ref[0], ses_ref[0]
    wnear[0, 0:1, :] = w0
    wnear[0, 1:2, :] = w1
    msrc[0:1, :] = jnp.full((1, 128), length, jnp.int32)
    msrc[1:2, :] = jnp.full((1, 128), session, jnp.int32)

    def tell(rel):
        return pltpu.make_async_remote_copy(
            src_ref=wnear.at[0], dst_ref=wnear.at[rel], send_sem=out_sem.at[1], recv_sem=table_sem.at[0],
            device_id={"tile": near(rel)}, device_id_type=MESH)

    def tell_far(i, far):
        dst = wfar.at[pl.ds((i ^ 1) * 4 + 8 * far, 4)]
        return pltpu.make_async_remote_copy(
            src_ref=wfar.at[pl.ds((i ^ 1) * 4, 4)] if far else wnear, dst_ref=dst,
            send_sem=out_sem.at[2], recv_sem=table_sem.at[5 if far else 1],
            device_id={"tile": (up, dn)[i]}, device_id_type=MESH)

    def meta(side):
        return pltpu.make_async_remote_copy(
            src_ref=msrc, dst_ref=mrecv.at[side], send_sem=out_sem.at[3], recv_sem=table_sem.at[2],
            device_id={"tile": (right, left)[side]}, device_id_type=MESH)

    for rel in range(1, 4):
        tell(rel).start()

    loads[0].wait()
    loads[1].wait()

    def square_row(ref):
        part = jnp.zeros((cap, HEAD_DIM), F32)
        for c in range(heads):
            x = ref[:, c * HEAD_DIM : (c + 1) * HEAD_DIM].astype(F32)
            part = part + x * x
        return jnp.sum(part.T, axis=0, keepdims=True)

    ssrc[0:1, :] = square_row(qr)
    ssrc[1:2, :] = square_row(kr)
    sbuf[h // 2] = ssrc[...]

    def share(i):
        return pltpu.make_async_remote_copy(
            src_ref=ssrc, dst_ref=sbuf.at[h // 2], send_sem=out_sem.at[4], recv_sem=table_sem.at[3],
            device_id={"head": lax.rem(h + 2 * i, nh)}, device_id_type=MESH)

    for i in range(1, nh // 2):
        share(i).start()

    pair = pltpu.make_async_remote_copy(
        src_ref=shalf, dst_ref=sother, send_sem=out_sem.at[5], recv_sem=table_sem.at[4],
        device_id={"head": hpair}, device_id_type=MESH)

    for i in range(heads):
        acc[i] = jnp.zeros((cap, HEAD_DIM), F32)
        mx[i] = jnp.full((cap, HEAD_DIM), NEG, F32)
        ls[i] = jnp.zeros((cap, HEAD_DIM), F32)

    @pl.when(t == 0)
    def _():
        ekv[0] = jnp.zeros((2, EDGE, wid), BF16)

    @pl.when(t == tiles - 1)
    def _():
        ekv[1] = jnp.zeros((2, EDGE, wid), BF16)

    landed(wnear.at[pl.ds(1, 3)], table_sem.at[0])
    copy = pltpu.make_async_copy(wnear, snear, tab_loc.at[0])
    copy.start()
    for i in range(2):
        tell_far(i, False).start()
    copy.wait()

    def edge(side, x):
        src = (tail.at[x], (kn, vr)[x].at[pl.ds(0, EDGE)])[side]
        return pltpu.make_async_remote_copy(
            src_ref=src, dst_ref=ekv.at[side, x], send_sem=edge_out.at[side], recv_sem=edge_in.at[side],
            device_id={"tile": (right, left)[side]}, device_id_type=MESH)

    def normalise():
        pair.wait_recv()
        loads[5].wait()
        loads[6].wait()
        factor = lax.rsqrt((shalf[...] + sother[...]) / width + EPSILON)
        for row, (raw, gain, out) in enumerate(((kr, gk_ref, kn), (qr, gq_ref, qn))):
            row = 1 - row
            wide = jnp.broadcast_to(factor[row : row + 1], (HEAD_DIM, cap)).T
            for c in range(heads):
                cols = slice(c * HEAD_DIM, (c + 1) * HEAD_DIM)
                out[:, cols] = (raw[:, cols].astype(F32) * wide * gain[cols].reshape(1, HEAD_DIM)).astype(BF16)
        loads[4].wait()
        place = lax.broadcasted_iota(jnp.int32, (EDGE, cap), 0) + (length - EDGE)
        pick = (lax.broadcasted_iota(jnp.int32, (EDGE, cap), 1) == place).astype(F32).astype(BF16)
        tail[0] = jnp.dot(pick, kn[...], preferred_element_type=F32).astype(BF16)
        tail[1] = jnp.dot(pick, vr[...], preferred_element_type=F32).astype(BF16)

        @pl.when(t < tiles - 1)
        def _():
            for x in range(2):
                edge(0, x).start()

        @pl.when(t > 0)
        def _():
            for x in range(2):
                edge(1, x).start()

    def spread(x, width):
        parts = [x] * (width // HEAD_DIM) + ([x[:, : width % HEAD_DIM]] if width % HEAD_DIM else [])
        return parts[0] if len(parts) == 1 else jnp.concatenate(parts, 1)

    def update(i, keys, values, bias):
        cols = pl.ds(pl.multiple_of(i * HEAD_DIM, HEAD_DIM), HEAD_DIM)
        scores = lax.dot_general(qn[:, cols], keys(cols), (((1,), (1,)), ((), ())), preferred_element_type=F32)
        scores = scores * SCORE_SCALE + bias
        before = mx[i]
        now = jnp.maximum(before, jnp.max(scores, axis=1, keepdims=True))
        expo = jnp.exp2(scores - spread(now, scores.shape[1]))
        keep = jnp.exp2(before - now)
        mx[i] = now
        ls[i] = ls[i] * keep + jnp.sum(expo, axis=1, keepdims=True)
        acc[i] = acc[i] * keep + jnp.dot(expo.astype(BF16), values(cols), preferred_element_type=F32)

    def own_attention(i):
        spot = lax.broadcasted_iota(jnp.int32, (1, cap), 1)
        ok_own = jnp.where(spot < length, 0.0, NEG).astype(F32)
        slot = lax.broadcasted_iota(jnp.int32, (1, 2 * EDGE), 1)
        ll, lsess = mrecv[0, 0:1, :], mrecv[0, 1:2, :]
        rl, rsess = mrecv[1, 0:1, :], mrecv[1, 1:2, :]
        from_left = (slot < EDGE) & (lsess == jnp.where(t > 0, session, -1)) & (slot >= EDGE - ll)
        from_right = (slot >= EDGE) & (rsess == jnp.where(t < tiles - 1, session, -1)) & (slot - EDGE < rl)
        ok_edge = jnp.where(from_left | from_right, 0.0, NEG).astype(F32)
        update(
            i,
            lambda c: jnp.concatenate([kn[:, c], ekv[0, 0, :, c], ekv[1, 0, :, c]], 0),
            lambda c: jnp.concatenate([vr[:, c], ekv[0, 1, :, c], ekv[1, 1, :, c]], 0),
            jnp.concatenate([ok_own, ok_edge], 1),
        )

    def origin(r):
        return lax.rem(z + nz - r, nz)

    def hand_out(r, x, src, rels=(2, 3, 1, 0)):
        owner = origin(r) * 4 + sub
        for rel in rels:
            out = (mkk, mvv)[x].at[r, pl.ds(0, 2)] if rel == 0 else sel.at[(x * 3 + rel - 1) * nz + r]
            for slot in range(2):
                out[slot] = src[jnp.maximum(snear[rel, slot, owner], 0)]
            if rel > 0:
                pltpu.make_async_remote_copy(
                    src_ref=sel.at[(x * 3 + rel - 1) * nz + r], dst_ref=(mkk, mvv)[x].at[r, pl.ds(2 * rel, 2)],
                    send_sem=out_sem.at[6], recv_sem=near_sem.at[r],
                    device_id={"tile": near(rel)}, device_id_type=MESH).start()

    def far_out(d, x, src, rels):
        owner = origin(full if d == 0 else nz - full) * 4 + sub
        for far_by in (2, 1) if d == x else (1,):
            i, r = (far_by - 1) * 2 + d, (full + far_by) if d == 0 else nz - full - far_by
            for rel in rels:
                place = (d * 2 + x if far_by == 1 else 4 + d) * 4 + rel
                for slot in range(2):
                    far[place, slot] = src[jnp.maximum(sfar[i * 4 + rel, slot, owner], 0)]
                pltpu.make_async_remote_copy(
                    src_ref=far.at[place], dst_ref=(mkk, mvv)[x].at[r, pl.ds(2 * rel, 2)],
                    send_sem=out_sem.at[7], recv_sem=near_sem.at[r],
                    device_id={"tile": at(steps[i], rel)}, device_id_type=MESH).start()

    def chunk(slots, beyond, loop):
        for r in slots:
            away = beyond and isinstance(r, int) and full < r < nz - full
            landed(sel.at[pl.ds(0, 8 if away else 6)], near_sem.at[r])
        group = lane // 8
        biases = []
        for pair_of in (slots[i : i + 2] for i in range(0, len(slots), 2)):
            bias = jnp.full((1, 128), NEG, F32)
            for j, r in enumerate(pair_of):
                for rel in range(4):
                    for slot in range(2):
                        want = snear[0, slot, origin(r) * 4 + near(rel) - z * 4]
                        miss = jnp.where(want < 0, NEG, 0.0).astype(F32)
                        bias = jnp.where(group == j * 8 + rel * 2 + slot, miss, bias)
            biases.append(bias[:, : 64 * len(pair_of)])
        bias = biases[0] if len(biases) == 1 else jnp.concatenate(biases, 1)

        def rows(ref, c):
            return jnp.concatenate([ref[r, :, :, c].reshape(64, HEAD_DIM) for r in slots], 0)

        def one(i):
            update(i, lambda c: rows(mkk, c), lambda c: rows(mvv, c), bias)

        if loop:
            pl.loop(0, heads)(one)
            return
        live = lax.broadcasted_iota(jnp.int32, (cap, HEAD_DIM), 0) < length
        for some in LAST_GROUPS:
            cols = [slice(i * HEAD_DIM, (i + 1) * HEAD_DIM) for i in some]
            scores = [
                lax.dot_general(qn[:, c], rows(mkk, c), (((1,), (1,)), ((), ())), preferred_element_type=F32)
                * SCORE_SCALE + bias for c in cols
            ]
            now = [jnp.maximum(mx[i], jnp.max(x, axis=1, keepdims=True)) for i, x in zip(some, scores)]
            expo = [jnp.exp2(x - spread(n, x.shape[1])) for x, n in zip(scores, now)]
            keep = [jnp.exp2(mx[i] - n) for i, n in zip(some, now)]
            whole = [ls[i] * k + jnp.sum(e, axis=1, keepdims=True) for i, k, e in zip(some, keep, expo)]
            for i, c, k, e, w in zip(some, cols, keep, expo, whole):
                out = acc[i] * k + jnp.dot(e.astype(BF16), rows(mvv, c), preferred_element_type=F32)
                o_ref[:, c] = jnp.where(live, out / w, 0.0).astype(BF16)

    cur_ka[...] = kvb[0]
    cur_va[...] = kvb[nz]
    hand_out(0, 0, cur_ka)
    hand_out(0, 1, cur_va)

    def arrived(s, x):
        for d in range(2):
            hop(d, s, x).wait_recv()
            hop(d, s + 1, x).start()

    def take(s, x):
        up_cur, dn_cur = ((cur_ka, cur_kb), (cur_va, cur_vb))[x]
        up_cur[...] = kvb[x * nz + s]
        dn_cur[...] = kvb[x * nz + nz - s]
        hand_out(s, x, up_cur)
        hand_out(nz - s, x, dn_cur)

    def halves():
        landed(sbuf.at[pl.ds(0, nh // 2 - 1)], table_sem.at[3])
        total = sbuf[0]
        for i in range(1, nh // 2):
            total = total + sbuf[i]
        shalf[...] = total
        pair.start()

    arrived(1, 0)
    take(1, 0)
    halves()
    arrived(1, 1)
    landed(wfar.at[pl.ds(0, 8)], table_sem.at[1])
    for i in range(2):
        tell_far(i, True).start()
    meta(0).start()
    meta(1).start()
    take(1, 1)
    arrived(2, 0)
    take(2, 0)
    normalise()
    arrived(2, 1)
    take(2, 1)
    chunk((1, nz - 1), False, True)
    @pl.loop(3, full)
    def _(s):
        arrived(s, 0)
        take(s, 0)
        pl.when(s == 3)(lambda: chunk((0,), False, True))
        arrived(s, 1)
        take(s, 1)
        chunk((s - 1, nz - s + 1), False, True)

    landed(wfar.at[pl.ds(8, 8)], table_sem.at[5])
    copy = pltpu.make_async_copy(wfar, sfar, tab_loc.at[1])
    copy.start()
    copy.wait()
    for x, (up_cur, dn_cur) in enumerate(((cur_ka, cur_kb), (cur_va, cur_vb))):
        hop(0, full, x).wait_recv()
        hop(1, full, x).wait_recv()
        up_cur[...] = kvb[x * nz + full]
        dn_cur[...] = kvb[x * nz + nz - full]
        far_out(0, x, up_cur, (2, 3))
        far_out(1, x, dn_cur, (2, 3))
        far_out(0, x, up_cur, (0, 1))
        far_out(1, x, dn_cur, (0, 1))
        hand_out(full, x, up_cur)
        hand_out(nz - full, x, dn_cur)
    chunk((full - 1, nz - full + 1), False, True)
    landed(mrecv, table_sem.at[2])
    for side, there in ((0, t > 0), (1, t < tiles - 1)):

        @pl.when(there)
        def _(side=side):
            landed(ekv.at[side], edge_in.at[side])

    for i in range(heads):
        own_attention(i)
    chunk((full, nz - full, half - 1, nz - half + 1, half), True, False)
    landed(kvb.at[pl.ds(0, 4 * full)], out_sem.at[0])
    landed(wnear.at[pl.ds(0, 3)], out_sem.at[1])
    landed(wfar, out_sem.at[2])
    landed(mrecv, out_sem.at[3])
    landed(sbuf.at[pl.ds(0, nh // 2 - 1)], out_sem.at[4])
    pair.wait_send()
    landed(sel.at[pl.ds(0, 6 * (2 * full + 1))], out_sem.at[6])
    landed(far, out_sem.at[7])
    for side, there in ((0, t < tiles - 1), (1, t > 0)):

        @pl.when(there)
        def _(side=side):
            landed(ekv.at[side], edge_out.at[side])


def per_device(tiles, nh, width, q, k, v, gq, gk, mk, mv, tile_len, session, owner, index):
    nz, half = tiles // 4, tiles // 8
    (cap, wid), (blocks, rows, _) = q.shape, mk.shape
    heads = wid // HEAD_DIM
    smem = pl.BlockSpec(memory_space=pltpu.SMEM)
    vmem = pl.BlockSpec(memory_space=pltpu.VMEM)
    hbm = pl.BlockSpec(memory_space=pltpu.HBM)
    sem = pltpu.SemaphoreType.DMA
    tile = pltpu.VMEM((cap, wid), BF16)
    state = pltpu.VMEM((heads, cap, HEAD_DIM), F32)
    block = pltpu.VMEM((blocks, rows, wid), BF16)
    return pl.pallas_call(
        functools.partial(kernel, tiles, nh, width),
        out_shape=jax.ShapeDtypeStruct((cap, wid), BF16),
        in_specs=[smem] * 2 + [hbm] * 9,
        out_specs=vmem,
        scratch_shapes=[
            pltpu.VMEM((2 * nz, blocks, rows, wid), BF16),
            block, block, block, block,
            tile, tile, tile, tile, tile,
            pltpu.VMEM((wid,), F32),
            pltpu.VMEM((wid,), F32),
            pltpu.SMEM(index.shape, jnp.int32),
            pltpu.SMEM(index.shape, jnp.int32),
            pltpu.VMEM((2, cap), F32),
            pltpu.VMEM((nh // 2, 2, cap), F32),
            pltpu.VMEM((2, cap), F32),
            pltpu.VMEM((2, cap), F32),
            pltpu.VMEM((4, 2, 128), jnp.int32),
            pltpu.VMEM((16, 2, 128), jnp.int32),
            pltpu.VMEM((2, 128), jnp.int32),
            pltpu.VMEM((2, 2, 128), jnp.int32),
            pltpu.SMEM((4, 2, 128), jnp.int32),
            pltpu.SMEM((16, 2, 128), jnp.int32),
            pltpu.VMEM((2, EDGE, wid), BF16),
            pltpu.VMEM((2, 2, EDGE, wid), BF16),
            pltpu.VMEM((6 * nz, 2, rows, wid), BF16),
            pltpu.VMEM((24, 2, rows, wid), BF16),
            pltpu.VMEM((nz, 8, rows, wid), BF16),
            pltpu.VMEM((nz, 8, rows, wid), BF16),
            state, state, state,
            sem((8,)), sem((2, half - 2, 2)), sem((9,)), sem((6,)), sem((nz,)), sem((2,)), sem((2,)), sem((2,)),
        ],
        compiler_params=pltpu.CompilerParams(
            collective_id=0, has_side_effects=True, vmem_limit_bytes=44 * 1024 * 1024
        ),
        name="tile_attention",
    )(
        tile_len, session, *(pltpu.with_memory_space_constraint(a, pltpu.HBM) for a in (owner.reshape(-1), index, gq, gk, q, k, v, mk, mv)),
    )


def solution(mesh):
    in_specs = (
        P("tile", "head"),
        P("tile", "head"),
        P("tile", "head"),
        P("head"),
        P("head"),
        P("tile", None, "head"),
        P("tile", None, "head"),
        P("tile"),
        P("tile"),
        P("tile", None),
        P("tile"),
    )
    tiles, nh = mesh.shape["tile"], mesh.shape["head"]

    def whole(q, *rest):
        body = functools.partial(per_device, tiles, nh, q.shape[1])
        return jax.shard_map(
            body, mesh=mesh, in_specs=in_specs, out_specs=P("tile", "head"), check_vma=False
        )(q, *rest)

    return whole
```
